256 devices in a mesh: chan: 32 (over x, z), tile: 8 (over y, core).
Axes of the slice: x: 4, y: 4, z: 8, core: 2. Of those that a mesh axis runs over, the one named last changes fastest.
Arguments:
- voltage: float32 [2, 64, 512, 1024], P(None, 'tile', 'chan'), may hold values from -6 to 6
- fir_taps: float32 [4, 1024], replicated, may hold values from -3 to 3
- tile_slot: int32 [10], replicated, may hold values from 0 to 15, as said below
- tile_blocks: int32 [10, 2], replicated, may hold values from 0 to 3, as said below
Outputs:
- visibility: float32 [16, 1024, 2, 128, 128], P('tile', 'chan')
The draws below stay inside these ranges and needn't reach their ends.
Inputs may be any that keep to these rules, and one draw needn't show every extreme that they name: `tile_slot`: the values are distinct; slot g belongs to device g // 2 of the tile axis. Every device of the tile axis holds at least one tile and at most 2, some exactly 2, and a device's tiles fill its lowest slots. `tile_blocks`: the unordered pairs of the rows are the 10 pairs of blocks p <= q, each once; a row may name its pair in either order.
All inputs are finite; a program needn't handle non-finite values.
Results may differ from the reference program's by a relative error of at most 0.0001.
Values sent between devices are 32-bit elements; how exact they have to be, the bound alone decides.
A program may use at most 64 MiB of HBM per device.

```python
import jax
import jax.numpy as jnp
import numpy as np
from jax import lax

CHANNELS = 1024
BLOCK = 128
NB = 4
TAPS = 4
SPECTRA = 64
INPUTS = 512
TRI = 10
SLOTS = 2
SLOTS_ALL = 16


def draw_tile_slot(key, part):
    devices = SLOTS_ALL // SLOTS
    order = jax.random.permutation(jax.random.fold_in(key, 11), devices)
    ranks = jnp.arange(TRI, dtype=jnp.int32)
    return (order[ranks % devices] * SLOTS + ranks // devices).astype(jnp.int32)


def draw_tile_blocks(key, part):
    row_block, col_block = np.triu_indices(NB)
    block_pairs = jnp.stack([jnp.asarray(row_block, jnp.int32), jnp.asarray(col_block, jnp.int32)], axis=1)
    chosen = block_pairs[jax.random.permutation(jax.random.fold_in(key, 23), TRI)]
    swapped = jax.random.randint(jax.random.fold_in(key, 37), (TRI, 1), 0, 2)
    return jnp.where(swapped == 1, chosen[:, ::-1], chosen).astype(jnp.int32)


def shard_levels(rng, shape, cuts, low, high):
    def one(position, blocks):
        heights = jax.random.uniform(jax.random.fold_in(jax.random.fold_in(rng, 6), position), (blocks,), jnp.float32, low / len(cuts), high / len(cuts))
        return jnp.repeat(jnp.exp(heights), shape[position] // blocks).reshape((-1,) + (1,) * (len(shape) - position - 1))

    level = one(*cuts[0])
    for cut in cuts[1:]:
        level = level * one(*cut)
    return level


def scatter_about(key, shape, spread, reach, split=(), kind=jnp.bfloat16):
    entries = spread * jax.random.normal(key, shape, jnp.float32)
    if split:
        entries = entries * shard_levels(key, shape, split, -0.22, 0.18)
    return jnp.clip(entries, -reach, reach).astype(kind)


def setup_inputs(seed: int = 0) -> dict:
    streams_of = jax.random.split(jax.random.key(seed), 5)
    voltage = scatter_about(streams_of[0], (2, SPECTRA, INPUTS, CHANNELS), 1.0, 6.0, ((1, 8), (2, 32)), jnp.float32)
    fir_taps = scatter_about(streams_of[1], (TAPS, CHANNELS), 0.5, 3.0, (), jnp.float32)
    tile_slot = draw_tile_slot(jax.random.fold_in(streams_of[4], 71), 0)
    tile_blocks = draw_tile_blocks(jax.random.fold_in(streams_of[4], 71), 0)
    return {"voltage": voltage, "fir_taps": fir_taps, "tile_slot": tile_slot, "tile_blocks": tile_blocks}


def product(left_rows, right_rows):
    return jnp.einsum("csi,csj->cij", left_rows, right_rows, precision=lax.Precision.HIGHEST)


def reference(voltage, fir_taps, tile_slot, tile_blocks):
    tap_count = fir_taps.shape[0]
    padded = jnp.concatenate([voltage, jnp.zeros((2, tap_count - 1, INPUTS, CHANNELS), jnp.float32)], axis=1)
    filtered = jnp.zeros((2, SPECTRA, INPUTS, CHANNELS), jnp.float32)
    for tap_index in range(tap_count):
        filtered = filtered + fir_taps[tap_index][None, None, None, :] * padded[:, tap_index:tap_index + SPECTRA]
    spectrum = jnp.fft.fft(filtered[0] + 1j * filtered[1], axis=-1, norm="ortho")
    real_rows = jnp.transpose(jnp.real(spectrum), (2, 0, 1))
    imag_rows = jnp.transpose(jnp.imag(spectrum), (2, 0, 1))

    def place_tile(tile_index, visibility):
        row_block = tile_blocks[tile_index, 0]
        col_block = tile_blocks[tile_index, 1]
        left_real = lax.dynamic_slice_in_dim(real_rows, row_block * BLOCK, BLOCK, 2)
        left_imag = lax.dynamic_slice_in_dim(imag_rows, row_block * BLOCK, BLOCK, 2)
        right_real = lax.dynamic_slice_in_dim(real_rows, col_block * BLOCK, BLOCK, 2)
        right_imag = lax.dynamic_slice_in_dim(imag_rows, col_block * BLOCK, BLOCK, 2)
        real_vis = product(left_real, right_real) + product(left_imag, right_imag)
        imag_vis = product(left_imag, right_real) - product(left_real, right_imag)
        update = (jnp.stack([real_vis, imag_vis], axis=1) / SPECTRA)[None]
        zero_index = jnp.zeros((), jnp.int32)
        return lax.dynamic_update_slice(visibility, update, (tile_slot[tile_index], zero_index, zero_index, zero_index, zero_index))

    initial = jnp.zeros((SLOTS_ALL, CHANNELS, 2, BLOCK, BLOCK), jnp.float32)
    return lax.fori_loop(0, TRI, place_tile, initial)
```

```python
import functools
import math

import jax
import jax.numpy as jnp
import ml_dtypes
import numpy as np
from jax import lax
from jax.experimental import pallas as pl
from jax.experimental.pallas import tpu as pltpu
from jax.sharding import PartitionSpec as P

MESH = pl.DeviceIdType.MESH
BLOCK = 128
RADIX = 4
HALVES = 2


def dft_tables(channels, scale):
    inner = channels // RADIX
    k2 = np.arange(inner)
    f2 = np.arange(inner)
    tables = []
    for f1 in range(RADIX):
        phase = (k2[None, :] * (RADIX * f2[:, None] + f1)) % channels * (2.0 * math.pi / channels)
        both = np.concatenate([np.cos(phase), np.sin(phase)], axis=1) * scale
        head = both.astype(ml_dtypes.bfloat16)
        tail = (both - head.astype(np.float64)).astype(ml_dtypes.bfloat16)
        tables.append(np.stack([head, tail]))
    return np.stack(tables)


def head_tail(value):
    head = value.astype(jnp.bfloat16)
    return head, (value - head.astype(jnp.float32)).astype(jnp.bfloat16)


def turn_lanes(value):
    row = lax.broadcasted_iota(jnp.int32, value.shape, 0)
    lane = lax.broadcasted_iota(jnp.int32, value.shape, 1) // 16
    for bit in range(3):
        step = 1 << bit
        row_bit = (row // step) % 2
        lane_bit = (lane // step) % 2
        up = pltpu.roll(pltpu.roll(value, 16 * step, 1), 8 - step, 0)
        if bit == 2:
            down = up
        else:
            down = pltpu.roll(pltpu.roll(value, 128 - 16 * step, 1), step, 0)
        value = jnp.where(row_bit == lane_bit, value, jnp.where(row_bit == 0, up, down))
    return value


def turn_kernel(
    chans, tiles, v_hbm, taps_ref, tab_hbm, out_hbm,
    v, tab, u_head, u_tail, sbuf, rbuf, gbuf,
    load_sem, hist_sem, turn_send, turn_recv, y_send, y_recv, out_sem,
):
    c = lax.axis_index("chan")
    t = lax.axis_index("tile")
    chunks = sbuf.shape[0]

    barrier = pltpu.get_barrier_semaphore()

    @pl.loop(1, chans)
    def _(i):
        pl.semaphore_signal(barrier, inc=1, device_id=(lax.rem(c + i, chans), t), device_id_type=MESH)

    for step in (1, 2, tiles - 1, tiles - 2):
        pl.semaphore_signal(barrier, inc=1, device_id=(c, lax.rem(t + step, tiles)), device_id_type=MESH)

    up = lax.rem(t + 2, tiles)
    down = lax.rem(t + tiles - 2, tiles)
    far = lax.rem(t + 4, tiles)
    partner = t + 1 - 2 * lax.rem(t, 2)
    previous = lax.rem(t + tiles - 1, tiles)

    load_v = pltpu.make_async_copy(v_hbm, v.at[:, pl.ds(0, 8)], load_sem.at[0])
    load_tab = pltpu.make_async_copy(tab_hbm, tab, load_sem.at[1])
    load_v.start()
    load_tab.start()

    def filter_half(half):
        @pl.loop(0, 4)
        def _(s):
            for kb in range(2):
                part = []
                for k1 in range(RADIX):
                    lanes = pl.ds(k1 * 256 + kb * 128, 128)
                    for ri in range(2):
                        total = jnp.zeros((16, 128), jnp.float32)
                        for tap in range(4):
                            total = total + taps_ref[pl.ds(tap, 1), lanes] * v[ri, half * 4 + s + tap, :, lanes]
                        part.append(total)
                r = part[0::2]
                m = part[1::2]
                sum_r, sum_m = r[0] + r[2], m[0] + m[2]
                dif_r, dif_m = r[0] - r[2], m[0] - m[2]
                odd_r, odd_m = r[1] + r[3], m[1] + m[3]
                odf_r, odf_m = r[1] - r[3], m[1] - m[3]
                turned = (
                    (sum_r + odd_r, sum_m + odd_m),
                    (dif_r + odf_m, dif_m - odf_r),
                    (sum_r - odd_r, sum_m - odd_m),
                    (dif_r - odf_m, dif_m + odf_r),
                )
                row = pl.multiple_of(s * 16, 16)
                for f1 in range(RADIX):
                    re, im = turned[f1]
                    re_h, re_t = head_tail(re)
                    im_h, im_t = head_tail(im)
                    first = pl.ds(kb * 128, 128)
                    second = pl.ds(256 + kb * 128, 128)
                    u_head[f1, pl.ds(row, 16), first] = re_h
                    u_tail[f1, pl.ds(row, 16), first] = re_t
                    u_head[f1, pl.ds(row, 16), second] = im_h
                    u_tail[f1, pl.ds(row, 16), second] = im_t
                    u_head[f1, pl.ds(64 + row, 16), first] = im_h
                    u_tail[f1, pl.ds(64 + row, 16), first] = im_t
                    u_head[f1, pl.ds(64 + row, 16), second] = -re_h
                    u_tail[f1, pl.ds(64 + row, 16), second] = -re_t

    def transform(n):
        f1 = n % RADIX
        dims = (((1,), (1,)), ((), ()))
        dot = functools.partial(lax.dot_general, dimension_numbers=dims, preferred_element_type=jnp.float32)
        head, tail = u_head[f1], u_tail[f1]
        sbuf[n] = dot(tab[f1, 0], tail) + dot(tab[f1, 1], head) + dot(tab[f1, 0], head)

    def turn_copy(n, to):
        return pltpu.make_async_remote_copy(
            src_ref=sbuf.at[n, pl.ds(pl.multiple_of(to * 8, 8), 8)],
            dst_ref=rbuf.at[n, pl.ds(pl.multiple_of(c * 8, 8), 8)],
            send_sem=turn_send.at[n],
            recv_sem=turn_recv.at[n],
            device_id=(to, t),
            device_id_type=MESH,
        )

    def turn_start(n):
        @pl.loop(1, chans)
        def _(i):
            turn_copy(n, lax.rem(c + i, chans)).start()

    def turn_wait(n, sem):
        rows = pl.ds(0, (chans - 1) * 8)
        pltpu.make_async_copy(sbuf.at[n, rows], rbuf.at[n, rows], sem.at[n]).wait()

    def relay(n):
        turn_wait(n, turn_recv)
        mine = pl.ds(pl.multiple_of(c * 8, 8), 8)
        rbuf[n, mine] = sbuf[n, mine]

        @pl.loop(0, 8)
        def _(j):
            for a in range(4):
                gbuf[n, t, j, :, pl.ds(a * 128, 128)] = turn_lanes(rbuf[n, pl.ds(64 * a + j, 8, stride=8), :])

    def y_copy(n, block, to, send, recv):
        return pltpu.make_async_remote_copy(
            src_ref=gbuf.at[n, block],
            dst_ref=gbuf.at[n, block],
            send_sem=y_send.at[n, send],
            recv_sem=y_recv.at[n, recv],
            device_id=(c, to),
            device_id_type=MESH,
        )

    def own_copies(n):
        return [y_copy(n, t, up, 0, 0), y_copy(n, t, down, 1, 1), y_copy(n, t, partner, 2, 3)]

    def near_copies(n):
        across = y_copy(n, down, up, 3, 2) if n % 2 == 0 else y_copy(n, up, down, 3, 2)
        return [across, y_copy(n, down, partner, 4, 4), y_copy(n, up, partner, 5, 5)]

    def far_copies(n):
        return [y_copy(n, far, partner, 6, 6)]

    def start_own(n):
        for copy in own_copies(n):
            copy.start()

    def start_near(n):
        own = own_copies(n)
        own[0].wait_recv()
        own[1].wait_recv()
        for copy in near_copies(n):
            copy.start()

    def start_far(n):
        near_copies(n)[0].wait_recv()
        far_copies(n)[0].start()

    def finish(n):
        own_copies(n)[2].wait_recv()
        near = near_copies(n)
        near[1].wait_recv()
        near[2].wait_recv()
        far_copies(n)[0].wait_recv()
        pltpu.make_async_copy(gbuf.at[n], out_hbm.at[n], out_sem.at[n]).start()

    history = pltpu.make_async_remote_copy(
        src_ref=v_hbm.at[:, pl.ds(0, 3)],
        dst_ref=v.at[:, pl.ds(8, 3)],
        send_sem=hist_sem.at[0],
        recv_sem=hist_sem.at[1],
        device_id=(c, previous),
        device_id_type=MESH,
    )

    load_v.wait()
    filter_half(0)
    load_tab.wait()
    transform(0)
    pl.semaphore_wait(barrier, chans - 1 + 4)
    history.start()
    half_chunks = chunks // HALVES
    turn_start(0)
    for n in range(1, half_chunks):
        transform(n)
        turn_start(n)
    history.wait_recv()

    @pl.when(t == tiles - 1)
    def _():
        for ri in range(2):
            for frame in range(8, 11):
                v[ri, frame] = jnp.zeros(v.shape[2:], jnp.float32)

    filter_half(1)
    for n in range(half_chunks, chunks):
        transform(n)
        turn_start(n)
    for n in range(chunks + 3):
        if n < chunks:
            relay(n)
            start_own(n)
        if 0 <= n - 1 < chunks:
            start_near(n - 1)
        if 0 <= n - 2 < chunks:
            start_far(n - 2)
        if 0 <= n - 3 < chunks:
            finish(n - 3)
    history.wait_send()
    for n in range(chunks):
        turn_wait(n, turn_send)
        for copy in own_copies(n) + near_copies(n) + far_copies(n):
            copy.wait_send()
        pltpu.make_async_copy(gbuf.at[n], out_hbm.at[n], out_sem.at[n]).wait()


def gather_spectra(voltage, fir_taps, tables, chans, tiles):
    frames, inputs, samples = voltage.shape[1:]
    chunks = HALVES * RADIX
    f32 = jnp.float32
    return pl.pallas_call(
        functools.partial(turn_kernel, chans, tiles),
        out_shape=jax.ShapeDtypeStruct((chunks, tiles, 8, 8, 512), f32),
        in_specs=[
            pl.BlockSpec(memory_space=pl.ANY),
            pl.BlockSpec(memory_space=pltpu.VMEM),
            pl.BlockSpec(memory_space=pl.ANY),
        ],
        out_specs=pl.BlockSpec(memory_space=pl.ANY),
        scratch_shapes=[
            pltpu.VMEM((2, frames + 3, inputs, samples), f32),
            pltpu.VMEM(tables.shape, jnp.bfloat16),
            pltpu.VMEM((RADIX, 128, 512), jnp.bfloat16),
            pltpu.VMEM((RADIX, 128, 512), jnp.bfloat16),
            pltpu.VMEM((chunks, 256, 128), f32),
            pltpu.VMEM((chunks, 256, 128), f32),
            pltpu.VMEM((chunks, tiles, 8, 8, 512), f32),
            pltpu.SemaphoreType.DMA((2,)),
            pltpu.SemaphoreType.DMA((2,)),
            pltpu.SemaphoreType.DMA((chunks,)),
            pltpu.SemaphoreType.DMA((chunks,)),
            pltpu.SemaphoreType.DMA((chunks, 7)),
            pltpu.SemaphoreType.DMA((chunks, 7)),
            pltpu.SemaphoreType.DMA((chunks,)),
        ],
        compiler_params=pltpu.CompilerParams(collective_id=0, has_side_effects=True, vmem_limit_bytes=40 << 20),
        name="turn",
    )(voltage, fir_taps, tables)


def tile_kernel(slot_ref, blocks_ref, x_ref, o_ref):
    t = lax.axis_index("tile")
    tile_count = slot_ref.shape[0]
    step = x_ref.shape[3]
    sign = jnp.where(lax.broadcasted_iota(jnp.int32, (16, 8, BLOCK), 1) < 4, -1.0, 1.0)
    for slot in range(o_ref.shape[0]):
        found = jnp.int32(0)
        row_block = jnp.int32(0)
        col_block = jnp.int32(0)
        for r in range(tile_count):
            hit = (slot_ref[r] == t * o_ref.shape[0] + slot).astype(jnp.int32)
            found += hit
            row_block += hit * blocks_ref[r, 0]
            col_block += hit * blocks_ref[r, 1]
        rows = pl.ds(pl.multiple_of(row_block * BLOCK, BLOCK), BLOCK)
        cols = pl.ds(pl.multiple_of(col_block * BLOCK, BLOCK), BLOCK)

        @pl.when(found > 0)
        def _():
            @pl.loop(0, step)
            def _(j):
                left = x_ref[:, 0, :, j, :, rows].reshape(BLOCK, BLOCK)
                right = x_ref[:, 0, :, j, :, cols].reshape(16, 8, BLOCK)
                other = (pltpu.roll(right, 4, 1) * sign).reshape(BLOCK, BLOCK)
                right = right.reshape(BLOCK, BLOCK)
                both = jnp.concatenate([right, other], axis=1)
                left_head, left_tail = head_tail(left.T)
                both_head, both_tail = head_tail(both)
                dot = functools.partial(jnp.dot, preferred_element_type=jnp.float32)
                total = dot(left_tail, both_head) + dot(left_head, both_tail) + dot(left_head, both_head)
                o_ref[slot, j, 0, 0] = total[:, :BLOCK]
                o_ref[slot, j, 0, 1] = total[:, BLOCK:]

        @pl.when(found == 0)
        def _():
            o_ref[slot] = jnp.zeros(o_ref.shape[1:], jnp.float32)


def make_tiles(spectra, tile_slot, tile_blocks, slots, step=4):
    tiles = spectra.shape[1]
    spectra = spectra.reshape(HALVES, RADIX, tiles, 8, 8, 512)
    out = pl.pallas_call(
        tile_kernel,
        grid=(RADIX, 8 // step),
        out_shape=jax.ShapeDtypeStruct((slots, 8, RADIX, 2, BLOCK, BLOCK), jnp.float32),
        in_specs=[
            pl.BlockSpec(memory_space=pltpu.SMEM),
            pl.BlockSpec(memory_space=pltpu.SMEM),
            pl.BlockSpec((HALVES, 1, tiles, step, 8, 512), lambda f, j: (0, f, 0, j, 0, 0)),
        ],
        out_specs=pl.BlockSpec((slots, step, 1, 2, BLOCK, BLOCK), lambda f, j: (0, j, f, 0, 0, 0)),
        compiler_params=pltpu.CompilerParams(vmem_limit_bytes=32 << 20),
        name="tiles",
    )(tile_slot, tile_blocks, spectra)
    return out.reshape(slots, 8 * RADIX, 2, BLOCK, BLOCK)


def solution(mesh):
    chans, tiles = mesh.shape["chan"], mesh.shape["tile"]

    def body(voltage, fir_taps, tile_slot, tile_blocks):
        channels = voltage.shape[3]
        spectra_total = voltage.shape[1] * tiles
        slots = -(-tile_slot.shape[0] // tiles)
        tables = jnp.asarray(dft_tables(channels, 1.0 / math.sqrt(channels * spectra_total)))
        spectra = gather_spectra(voltage, fir_taps, tables, chans, tiles)
        return make_tiles(spectra, tile_slot, tile_blocks, slots)

    in_specs = (P(None, "tile", "chan", None), P(), P(), P())
    out_specs = P("tile", "chan", None, None, None)
    return jax.shard_map(body, mesh=mesh, in_specs=in_specs, out_specs=out_specs, check_vma=False)
```

```python
import functools
import math

import jax
import jax.numpy as jnp
import ml_dtypes
import numpy as np
from jax import lax
from jax.experimental import pallas as pl
from jax.experimental.pallas import tpu as pltpu
from jax.sharding import PartitionSpec as P

MESH = pl.DeviceIdType.MESH
BLOCK = 128
RADIX = 4
HALVES = 2


def dft_tables(channels, scale):
    inner = channels // RADIX
    k2 = np.arange(inner)
    f2 = np.arange(inner)
    tables = []
    for f1 in range(RADIX):
        phase = (k2[None, :] * (RADIX * f2[:, None] + f1)) % channels * (2.0 * math.pi / channels)
        both = np.concatenate([np.cos(phase), np.sin(phase)], axis=1) * scale
        head = both.astype(ml_dtypes.bfloat16)
        tail = (both - head.astype(np.float64)).astype(ml_dtypes.bfloat16)
        tables.append(np.stack([head, tail]))
    return np.stack(tables)


def head_tail(value):
    head = value.astype(jnp.bfloat16)
    return head, (value - head.astype(jnp.float32)).astype(jnp.bfloat16)


def turn_lanes(value):
    row = lax.broadcasted_iota(jnp.int32, value.shape, 0)
    lane = lax.broadcasted_iota(jnp.int32, value.shape, 1) // 16
    for bit in range(3):
        step = 1 << bit
        row_bit = (row // step) % 2
        lane_bit = (lane // step) % 2
        up = pltpu.roll(pltpu.roll(value, 16 * step, 1), 8 - step, 0)
        if bit == 2:
            down = up
        else:
            down = pltpu.roll(pltpu.roll(value, 128 - 16 * step, 1), step, 0)
        value = jnp.where(row_bit == lane_bit, value, jnp.where(row_bit == 0, up, down))
    return value


def find_tile(slot_ref, blocks_ref, wanted):
    found = jnp.int32(0)
    row_block = jnp.int32(0)
    col_block = jnp.int32(0)
    for r in range(slot_ref.shape[0]):
        hit = (slot_ref[r] == wanted).astype(jnp.int32)
        found += hit
        row_block += hit * blocks_ref[0, r]
        col_block += hit * blocks_ref[1, r]
    rows = pl.ds(pl.multiple_of(row_block * BLOCK, BLOCK), BLOCK)
    cols = pl.ds(pl.multiple_of(col_block * BLOCK, BLOCK), BLOCK)
    return found, rows, cols


def pick_weights(slot_ref, blocks_ref, wanted, side, blocks):
    weights = [jnp.float32(0)] * blocks
    for r in range(slot_ref.shape[0]):
        hit = slot_ref[r] == wanted
        for block in range(blocks):
            weights[block] += jnp.where(hit & (blocks_ref[side, r] == block), 1.0, 0.0)
    return weights


def correlate(left, right):
    sign = jnp.where(lax.broadcasted_iota(jnp.int32, (16, 8, BLOCK), 1) < 4, -1.0, 1.0)
    left = left.reshape(BLOCK, BLOCK)
    other = (pltpu.roll(right, 4, 1) * sign).reshape(BLOCK, BLOCK)
    both = jnp.concatenate([right.reshape(BLOCK, BLOCK), other], axis=1)
    left_head, left_tail = head_tail(left.T)
    both_head, both_tail = head_tail(both)
    dot = functools.partial(jnp.dot, preferred_element_type=jnp.float32)
    return dot(left_tail, both_head) + dot(left_head, both_tail) + dot(left_head, both_head)


def turn_kernel(
    chans, tiles, slots, v_hbm, taps_hbm, tab_hbm, slot_ref, blocks_ref, out_hbm, last_ref,
    v, taps_ref, tab, u_head, u_tail, sbuf, rbuf, staged, *rest,
):
    gbufs = rest[: HALVES * RADIX]
    load_sem, hist_sem, turn_send, turn_recv, y_send, y_recv, out_sem = rest[HALVES * RADIX :]
    c = lax.axis_index("chan")
    t = lax.axis_index("tile")
    chunks = sbuf.shape[0]

    barrier = pltpu.get_barrier_semaphore()

    @pl.loop(1, chans)
    def _(i):
        pl.semaphore_signal(barrier, inc=1, device_id=(lax.rem(c + i, chans), t), device_id_type=MESH)

    for step in (1, 2, tiles - 1, tiles - 2):
        pl.semaphore_signal(barrier, inc=1, device_id=(c, lax.rem(t + step, tiles)), device_id_type=MESH)

    up = lax.rem(t + 2, tiles)
    down = lax.rem(t + tiles - 2, tiles)
    far = lax.rem(t + 4, tiles)
    partner = t + 1 - 2 * lax.rem(t, 2)
    previous = lax.rem(t + tiles - 1, tiles)

    load_v = pltpu.make_async_copy(v_hbm, v.at[:, pl.ds(0, 8)], load_sem.at[0])
    load_tab = pltpu.make_async_copy(tab_hbm, tab, load_sem.at[1])
    load_taps = pltpu.make_async_copy(taps_hbm, taps_ref, load_sem.at[2])
    load_v.start()
    load_taps.start()
    load_tab.start()

    weights = [
        [pick_weights(slot_ref, blocks_ref, t * slots + slot, side, 4) for side in range(2)] for slot in range(slots)
    ]

    def filter_half(half):
        @pl.loop(0, 4)
        def _(s):
            for kb in range(2):
                part = []
                for k1 in range(RADIX):
                    lanes = pl.ds(k1 * 256 + kb * 128, 128)
                    for ri in range(2):
                        total = jnp.zeros((16, 128), jnp.float32)
                        for tap in range(4):
                            total = total + taps_ref[pl.ds(tap, 1), lanes] * v[ri, half * 4 + s + tap, :, lanes]
                        part.append(total)
                r = part[0::2]
                m = part[1::2]
                sum_r, sum_m = r[0] + r[2], m[0] + m[2]
                dif_r, dif_m = r[0] - r[2], m[0] - m[2]
                odd_r, odd_m = r[1] + r[3], m[1] + m[3]
                odf_r, odf_m = r[1] - r[3], m[1] - m[3]
                turned = (
                    (sum_r + odd_r, sum_m + odd_m),
                    (dif_r + odf_m, dif_m - odf_r),
                    (sum_r - odd_r, sum_m - odd_m),
                    (dif_r - odf_m, dif_m + odf_r),
                )
                row = pl.multiple_of(s * 16, 16)
                for f1 in range(RADIX):
                    re, im = turned[f1]
                    re_h, re_t = head_tail(re)
                    im_h, im_t = head_tail(im)
                    first = pl.ds(kb * 128, 128)
                    second = pl.ds(256 + kb * 128, 128)
                    u_head[f1, pl.ds(row, 16), first] = re_h
                    u_tail[f1, pl.ds(row, 16), first] = re_t
                    u_head[f1, pl.ds(row, 16), second] = im_h
                    u_tail[f1, pl.ds(row, 16), second] = im_t
                    u_head[f1, pl.ds(64 + row, 16), first] = im_h
                    u_tail[f1, pl.ds(64 + row, 16), first] = im_t
                    u_head[f1, pl.ds(64 + row, 16), second] = -re_h
                    u_tail[f1, pl.ds(64 + row, 16), second] = -re_t

    def transform(n):
        f1 = n % RADIX
        dims = (((1,), (1,)), ((), ()))
        dot = functools.partial(lax.dot_general, dimension_numbers=dims, preferred_element_type=jnp.float32)
        head, tail = u_head[f1], u_tail[f1]
        sbuf[n] = dot(tab[f1, 0], tail) + dot(tab[f1, 1], head) + dot(tab[f1, 0], head)

    def turn_copy(n, to):
        return pltpu.make_async_remote_copy(
            src_ref=sbuf.at[n, pl.ds(pl.multiple_of(to * 8, 8), 8)],
            dst_ref=rbuf.at[n, pl.ds(pl.multiple_of(c * 8, 8), 8)],
            send_sem=turn_send.at[n],
            recv_sem=turn_recv.at[n],
            device_id=(to, t),
            device_id_type=MESH,
        )

    def turn_start(n):
        @pl.loop(1, chans)
        def _(i):
            turn_copy(n, lax.rem(c + i, chans)).start()

    def turn_wait(n, sem):
        rows = pl.ds(0, (chans - 1) * 8)
        pltpu.make_async_copy(sbuf.at[n, rows], rbuf.at[n, rows], sem.at[n]).wait()

    def relay(n):
        turn_wait(n, turn_recv)
        mine = pl.ds(pl.multiple_of(c * 8, 8), 8)
        rbuf[n, mine] = sbuf[n, mine]

        for j in range(8):
            for a in range(4):
                gbufs[n][t, j, :, pl.ds(a * 128, 128)] = turn_lanes(rbuf[n, pl.ds(64 * a + j, 8, stride=8), :])

    def y_copy(n, block, to, send, recv):
        return pltpu.make_async_remote_copy(
            src_ref=gbufs[n].at[block],
            dst_ref=gbufs[n].at[block],
            send_sem=y_send.at[n, send],
            recv_sem=y_recv.at[n, recv],
            device_id=(c, to),
            device_id_type=MESH,
        )

    def own_copies(n):
        return [y_copy(n, t, up, 0, 0), y_copy(n, t, down, 1, 1), y_copy(n, t, partner, 2, 3)]

    def near_copies(n):
        across = y_copy(n, down, up, 3, 2) if n % 2 == 0 else y_copy(n, up, down, 3, 2)
        return [across, y_copy(n, down, partner, 4, 4), y_copy(n, up, partner, 5, 5)]

    def far_copies(n):
        return [y_copy(n, far, partner, 6, 6)]

    def start_own(n):
        for copy in own_copies(n):
            copy.start()

    def start_near(n):
        own = own_copies(n)
        own[0].wait_recv()
        own[1].wait_recv()
        for copy in near_copies(n):
            copy.start()

    def start_far(n):
        near_copies(n)[0].wait_recv()
        far_copies(n)[0].start()

    def finish(n):
        own_copies(n)[2].wait_recv()
        near = near_copies(n)
        near[1].wait_recv()
        near[2].wait_recv()
        far_copies(n)[0].wait_recv()

    def out_copy(f1):
        return pltpu.make_async_copy(staged.at[f1], out_hbm.at[f1], out_sem.at[f1])

    def last_copy(half):
        n = half * RADIX + RADIX - 1
        return pltpu.make_async_copy(gbufs[n], last_ref.at[half], out_sem.at[n])

    def make_tiles(f1):
        halves = [gbufs[half * RADIX + f1] for half in range(HALVES)]

        @pl.loop(0, 8, step=2)
        def _(first):
            for more in range(2):
                j = first + more
                blocks = [
                    jnp.concatenate([half[:, j, :, block * BLOCK : (block + 1) * BLOCK] for half in halves], axis=0)
                    for block in range(4)
                ]
                for slot in range(slots):
                    left, right = [sum(w * x for w, x in zip(side, blocks)) for side in weights[slot]]
                    total = correlate(left, right)
                    staged[f1, slot, j, 0] = total[:, :BLOCK]
                    staged[f1, slot, j, 1] = total[:, BLOCK:]

        out_copy(f1).start()

    history = pltpu.make_async_remote_copy(
        src_ref=v_hbm.at[:, pl.ds(0, 3)],
        dst_ref=v.at[:, pl.ds(8, 3)],
        send_sem=hist_sem.at[0],
        recv_sem=hist_sem.at[1],
        device_id=(c, previous),
        device_id_type=MESH,
    )

    load_v.wait()
    load_taps.wait()
    filter_half(0)
    load_tab.wait()
    transform(0)
    pl.semaphore_wait(barrier, chans - 1 + 4)
    history.start()
    half_chunks = chunks // HALVES
    turn_start(0)
    for n in range(1, half_chunks):
        transform(n)
        turn_start(n)
    relay(0)
    start_own(0)
    history.wait_recv()

    @pl.when(t == tiles - 1)
    def _():
        for ri in range(2):
            for frame in range(8, 11):
                v[ri, frame] = jnp.zeros(v.shape[2:], jnp.float32)

    filter_half(1)
    for n in range(half_chunks, chunks):
        transform(n)
        turn_start(n)
    for n in range(1, chunks + 3):
        if n < chunks:
            relay(n)
            start_own(n)
        if 0 <= n - 1 < chunks:
            start_near(n - 1)
        if 0 <= n - 2 < chunks:
            start_far(n - 2)
        done = n - 3
        if 0 <= done < chunks:
            finish(done)
            half, f1 = done // RADIX, done % RADIX
            if f1 == RADIX - 1:
                last_copy(half).start()
            elif half == HALVES - 1:
                make_tiles(f1)
    history.wait_send()
    for n in range(chunks):
        turn_wait(n, turn_send)
        for copy in own_copies(n) + near_copies(n) + far_copies(n):
            copy.wait_send()
    for f1 in range(RADIX - 1):
        out_copy(f1).wait()
    for half in range(HALVES):
        last_copy(half).wait()


def early_tiles(voltage, fir_taps, tables, tile_slot, tile_blocks, chans, tiles, slots):
    frames, inputs, samples = voltage.shape[1:]
    chunks = HALVES * RADIX
    f32 = jnp.float32
    any_space = pl.BlockSpec(memory_space=pl.ANY)
    smem = pl.BlockSpec(memory_space=pltpu.SMEM)
    return pl.pallas_call(
        functools.partial(turn_kernel, chans, tiles, slots),
        out_shape=(
            jax.ShapeDtypeStruct((RADIX - 1, slots, 8, 2, BLOCK, BLOCK), f32),
            jax.ShapeDtypeStruct((HALVES, tiles, 8, 8, 512), f32),
        ),
        in_specs=[any_space, any_space, any_space, smem, smem],
        out_specs=(any_space, any_space),
        scratch_shapes=[
            pltpu.VMEM((2, frames + 3, inputs, samples), f32),
            pltpu.VMEM(fir_taps.shape, f32),
            pltpu.VMEM(tables.shape, jnp.bfloat16),
            pltpu.VMEM((RADIX, 128, 512), jnp.bfloat16),
            pltpu.VMEM((RADIX, 128, 512), jnp.bfloat16),
            pltpu.VMEM((chunks, 256, 128), f32),
            pltpu.VMEM((chunks, 256, 128), f32),
            pltpu.VMEM((RADIX - 1, slots, 8, 2, BLOCK, BLOCK), f32),
            *[pltpu.VMEM((tiles, 8, 8, 512), f32) for _ in range(chunks)],
            pltpu.SemaphoreType.DMA((3,)),
            pltpu.SemaphoreType.DMA((2,)),
            pltpu.SemaphoreType.DMA((chunks,)),
            pltpu.SemaphoreType.DMA((chunks,)),
            pltpu.SemaphoreType.DMA((chunks, 7)),
            pltpu.SemaphoreType.DMA((chunks, 7)),
            pltpu.SemaphoreType.DMA((chunks,)),
        ],
        compiler_params=pltpu.CompilerParams(collective_id=0, has_side_effects=True, vmem_limit_bytes=67_043_328),
        name="turn",
    )(voltage, fir_taps, tables, tile_slot, tile_blocks)


def tile_kernel(slot_ref, blocks_ref, early_ref, spectra_ref, out_hbm, spectra, moved, staged, load_sem, move_sem, out_sem):
    t = lax.axis_index("tile")
    slots, step = staged.shape[:2]
    load = pltpu.make_async_copy(spectra_ref, spectra, load_sem)
    load.start()
    parts = [(f1, slot) for f1 in range(RADIX - 1) for slot in range(slots)]
    moves = [pltpu.make_async_copy(early_ref.at[f1, slot], moved.at[f1, slot], move_sem.at[f1, slot]) for f1, slot in parts]
    early = [pltpu.make_async_copy(moved.at[f1, slot], out_hbm.at[slot, :, f1], out_sem.at[f1, slot]) for f1, slot in parts]
    for move in moves:
        move.start()
    load.wait()
    halves = [spectra.at[half] for half in range(HALVES)]
    late = []
    ahead = len(parts) // slots
    for slot in range(slots):
        for move, copy in zip(moves[slot * ahead : (slot + 1) * ahead], early[slot * ahead : (slot + 1) * ahead]):
            move.wait()
            copy.start()
        found, rows, cols = find_tile(slot_ref, blocks_ref, t * slots + slot)

        @pl.when(found > 0)
        def _():
            @pl.loop(0, step, step=4)
            def _(first):
                for more in range(4):
                    j = first + more
                    left, right = [
                        jnp.concatenate([half[:, j, :, lanes] for half in halves], axis=0) for lanes in (rows, cols)
                    ]
                    total = correlate(left, right)
                    staged[slot, j, 0] = total[:, :BLOCK]
                    staged[slot, j, 1] = total[:, BLOCK:]

        @pl.when(found == 0)
        def _():
            staged[slot] = jnp.zeros(staged.shape[1:], jnp.float32)

        late.append(pltpu.make_async_copy(staged.at[slot], out_hbm.at[slot, :, RADIX - 1], out_sem.at[RADIX - 1, slot]))
        late[-1].start()
    for copy in early + late:
        copy.wait()


def last_tiles(early, spectra, tile_slot, tile_blocks):
    slots = early.shape[1]
    smem = pl.BlockSpec(memory_space=pltpu.SMEM)
    any_space = pl.BlockSpec(memory_space=pl.ANY)
    return pl.pallas_call(
        tile_kernel,
        out_shape=jax.ShapeDtypeStruct((slots, 8, RADIX, 2, BLOCK, BLOCK), jnp.float32),
        in_specs=[smem, smem, any_space, any_space],
        out_specs=any_space,
        scratch_shapes=[
            pltpu.VMEM(spectra.shape, jnp.float32),
            pltpu.VMEM(early.shape, jnp.float32),
            pltpu.VMEM((slots, 8, 2, BLOCK, BLOCK), jnp.float32),
            pltpu.SemaphoreType.DMA,
            pltpu.SemaphoreType.DMA((RADIX - 1, slots)),
            pltpu.SemaphoreType.DMA((RADIX, slots)),
        ],
        compiler_params=pltpu.CompilerParams(vmem_limit_bytes=67_043_328),
        name="tiles",
    )(tile_slot, tile_blocks, early, spectra)


def solution(mesh):
    chans, tiles = mesh.shape["chan"], mesh.shape["tile"]

    def body(voltage, fir_taps, tile_slot, tile_blocks):
        channels = voltage.shape[3]
        spectra_total = voltage.shape[1] * tiles
        slots = -(-tile_slot.shape[0] // tiles)
        blocks = tile_blocks.T
        tables = jnp.asarray(dft_tables(channels, 1.0 / math.sqrt(channels * spectra_total)))
        early, last = early_tiles(voltage, fir_taps, tables, tile_slot, blocks, chans, tiles, slots)
        out = last_tiles(early, last, tile_slot, blocks)
        return out.reshape(slots, 8 * RADIX, 2, BLOCK, BLOCK)

    in_specs = (P(None, "tile", "chan", None), P(), P(), P())
    out_specs = P("tile", "chan", None, None, None)
    return jax.shard_map(body, mesh=mesh, in_specs=in_specs, out_specs=out_specs, check_vma=False)
```

```python
import functools
import math

import jax
import jax.numpy as jnp
import ml_dtypes
import numpy as np
from jax import lax
from jax.experimental import pallas as pl
from jax.experimental.pallas import tpu as pltpu
from jax.sharding import PartitionSpec as P

MESH = pl.DeviceIdType.MESH
BLOCK = 128
RADIX = 4
TURN_LIMIT = 40 << 20
LAST_LIMIT = 40 << 20
HALVES = 2
AHEAD = 3


def dft_tables(channels, scale):
    inner = channels // RADIX
    k2 = np.arange(inner)
    f2 = np.arange(inner)
    tables = []
    for f1 in range(RADIX):
        phase = (k2[None, :] * (RADIX * f2[:, None] + f1)) % channels * (2.0 * math.pi / channels)
        both = np.concatenate([np.cos(phase), np.sin(phase)], axis=1) * scale
        head = both.astype(ml_dtypes.bfloat16)
        tail = (both - head.astype(np.float64)).astype(ml_dtypes.bfloat16)
        tables.append(np.stack([head, tail]))
    return np.stack(tables)


def head_tail(value):
    head = value.astype(jnp.bfloat16)
    return head, (value - head.astype(jnp.float32)).astype(jnp.bfloat16)


def turn_lanes(value):
    row = lax.broadcasted_iota(jnp.int32, value.shape, 0)
    lane = lax.broadcasted_iota(jnp.int32, value.shape, 1) // 16
    for bit in range(3):
        step = 1 << bit
        row_bit = (row // step) % 2
        lane_bit = (lane // step) % 2
        up = pltpu.roll(pltpu.roll(value, 16 * step, 1), 8 - step, 0)
        if bit == 2:
            down = up
        else:
            down = pltpu.roll(pltpu.roll(value, 128 - 16 * step, 1), step, 0)
        value = jnp.where(row_bit == lane_bit, value, jnp.where(row_bit == 0, up, down))
    return value


def find_tile(slot_ref, blocks_ref, wanted):
    found = jnp.int32(0)
    row_block = jnp.int32(0)
    col_block = jnp.int32(0)
    for r in range(slot_ref.shape[0]):
        hit = (slot_ref[r] == wanted).astype(jnp.int32)
        found += hit
        row_block += hit * blocks_ref[0, r]
        col_block += hit * blocks_ref[1, r]
    rows = pl.ds(pl.multiple_of(row_block * BLOCK, BLOCK), BLOCK)
    cols = pl.ds(pl.multiple_of(col_block * BLOCK, BLOCK), BLOCK)
    return found, rows, cols


def pick_weights(slot_ref, blocks_ref, wanted, side, blocks):
    weights = [jnp.float32(0)] * blocks
    for r in range(slot_ref.shape[0]):
        hit = slot_ref[r] == wanted
        for block in range(blocks):
            weights[block] += jnp.where(hit & (blocks_ref[side, r] == block), 1.0, 0.0)
    return weights


def correlate(left, right):
    sign = jnp.where(lax.broadcasted_iota(jnp.int32, (16, 8, BLOCK), 1) < 4, -1.0, 1.0)
    left = left.reshape(BLOCK, BLOCK)
    other = (pltpu.roll(right, 4, 1) * sign).reshape(BLOCK, BLOCK)
    both = jnp.concatenate([right.reshape(BLOCK, BLOCK), other], axis=1)
    left_head, left_tail = head_tail(left.T)
    both_head, both_tail = head_tail(both)
    dot = functools.partial(jnp.dot, preferred_element_type=jnp.float32)
    return dot(left_tail, both_head) + dot(left_head, both_tail) + dot(left_head, both_head)


def turn_kernel(
    chans, tiles, slots, v_hbm, taps_hbm, tab_hbm, slot_ref, blocks_ref, out_hbm, last_ref,
    v, taps_ref, tab, u_head, u_tail, sbuf, rbuf, staged, *rest,
):
    gbufs = rest[: HALVES * RADIX]
    load_sem, hist_sem, turn_send, turn_recv, y_send, y_recv, out_sem = rest[HALVES * RADIX :]
    c = lax.axis_index("chan")
    t = lax.axis_index("tile")
    chunks = sbuf.shape[0]

    barrier = pltpu.get_barrier_semaphore()

    @pl.loop(1, chans)
    def _(i):
        pl.semaphore_signal(barrier, inc=1, device_id=(lax.rem(c + i, chans), t), device_id_type=MESH)

    for step in (1, 2, tiles - 1, tiles - 2):
        pl.semaphore_signal(barrier, inc=1, device_id=(c, lax.rem(t + step, tiles)), device_id_type=MESH)

    up = lax.rem(t + 2, tiles)
    down = lax.rem(t + tiles - 2, tiles)
    far = lax.rem(t + 4, tiles)
    partner = t + 1 - 2 * lax.rem(t, 2)
    previous = lax.rem(t + tiles - 1, tiles)

    load_v = pltpu.make_async_copy(v_hbm, v.at[:, pl.ds(0, 8)], load_sem.at[0])
    load_tab = pltpu.make_async_copy(tab_hbm, tab, load_sem.at[1])
    load_taps = pltpu.make_async_copy(taps_hbm, taps_ref, load_sem.at[2])
    load_v.start()
    load_taps.start()
    load_tab.start()

    weights = [
        [pick_weights(slot_ref, blocks_ref, t * slots + slot, side, 4) for side in range(2)] for slot in range(slots)
    ]

    def filter_half(half):
        @pl.loop(0, 4)
        def _(s):
            for kb in range(2):
                part = []
                for k1 in range(RADIX):
                    lanes = pl.ds(k1 * 256 + kb * 128, 128)
                    for ri in range(2):
                        total = jnp.zeros((16, 128), jnp.float32)
                        for tap in range(4):
                            total = total + taps_ref[pl.ds(tap, 1), lanes] * v[ri, half * 4 + s + tap, :, lanes]
                        part.append(total)
                r = part[0::2]
                m = part[1::2]
                sum_r, sum_m = r[0] + r[2], m[0] + m[2]
                dif_r, dif_m = r[0] - r[2], m[0] - m[2]
                odd_r, odd_m = r[1] + r[3], m[1] + m[3]
                odf_r, odf_m = r[1] - r[3], m[1] - m[3]
                turned = (
                    (sum_r + odd_r, sum_m + odd_m),
                    (dif_r + odf_m, dif_m - odf_r),
                    (sum_r - odd_r, sum_m - odd_m),
                    (dif_r - odf_m, dif_m + odf_r),
                )
                row = pl.multiple_of(s * 16, 16)
                for f1 in range(RADIX):
                    re, im = turned[f1]
                    re_h, re_t = head_tail(re)
                    im_h, im_t = head_tail(im)
                    first = pl.ds(kb * 128, 128)
                    second = pl.ds(256 + kb * 128, 128)
                    u_head[f1, pl.ds(row, 16), first] = re_h
                    u_tail[f1, pl.ds(row, 16), first] = re_t
                    u_head[f1, pl.ds(row, 16), second] = im_h
                    u_tail[f1, pl.ds(row, 16), second] = im_t
                    u_head[f1, pl.ds(64 + row, 16), first] = im_h
                    u_tail[f1, pl.ds(64 + row, 16), first] = im_t
                    u_head[f1, pl.ds(64 + row, 16), second] = -re_h
                    u_tail[f1, pl.ds(64 + row, 16), second] = -re_t

    def transform(n):
        f1 = n % RADIX
        dims = (((1,), (1,)), ((), ()))
        dot = functools.partial(lax.dot_general, dimension_numbers=dims, preferred_element_type=jnp.float32)
        head, tail = u_head[f1], u_tail[f1]
        sbuf[n] = dot(tab[f1, 0], tail) + dot(tab[f1, 1], head) + dot(tab[f1, 0], head)

    def turn_copy(n, to):
        return pltpu.make_async_remote_copy(
            src_ref=sbuf.at[n, pl.ds(pl.multiple_of(to * 8, 8), 8)],
            dst_ref=rbuf.at[n, pl.ds(pl.multiple_of(c * 8, 8), 8)],
            send_sem=turn_send.at[n],
            recv_sem=turn_recv.at[n],
            device_id=(to, t),
            device_id_type=MESH,
        )

    def turn_start(n):
        turn_copy(n, lax.rem(c + chans // 2, chans)).start()

        @pl.loop(1, chans // 2)
        def _(i):
            turn_copy(n, lax.rem(c + i, chans)).start()
            turn_copy(n, lax.rem(c + chans - i, chans)).start()

    def turn_wait(n, sem):
        rows = pl.ds(0, (chans - 1) * 8)
        pltpu.make_async_copy(sbuf.at[n, rows], rbuf.at[n, rows], sem.at[n]).wait()

    def relay(n):
        turn_wait(n, turn_recv)
        mine = pl.ds(pl.multiple_of(c * 8, 8), 8)
        rbuf[n, mine] = sbuf[n, mine]

        for j in range(8):
            for a in range(4):
                gbufs[n][t, j, :, pl.ds(a * 128, 128)] = turn_lanes(rbuf[n, pl.ds(64 * a + j, 8, stride=8), :])

    def y_copy(n, block, to, slot, part=pl.ds(0, 8)):
        return pltpu.make_async_remote_copy(
            src_ref=gbufs[n].at[block, part],
            dst_ref=gbufs[n].at[block, part],
            send_sem=y_send.at[n, slot],
            recv_sem=y_recv.at[n, slot],
            device_id=(c, to),
            device_id_type=MESH,
        )

    low, high = pl.ds(0, 4), pl.ds(4, 4)

    def y_copies(n):
        return {
            "up low": y_copy(n, t, up, 0, low),
            "down high": y_copy(n, t, down, 1, high),
            "up high": y_copy(n, t, up, 2, high),
            "down low": y_copy(n, t, down, 3, low),
            "own": y_copy(n, t, partner, 4),
            "on low": y_copy(n, down, up, 5, low),
            "on high": y_copy(n, up, down, 6, high),
            "below": y_copy(n, down, partner, 7),
            "above": y_copy(n, up, partner, 8),
            "far": y_copy(n, far, partner, 9),
        }

    all_copies = [y_copies(n) for n in range(chunks)]

    def y_start(n, *names):
        for name in names:
            all_copies[n][name].start()

    def y_arrived(n, *names):
        for name in names:
            all_copies[n][name].wait_recv()

    def start_own(n):
        y_start(n, "up low", "down high", "up high", "down low", "own")

    def start_near(n):
        y_arrived(n, "up low")
        y_start(n, "on low")
        y_arrived(n, "down high")
        y_start(n, "on high")

    def start_far(n):
        y_arrived(n, "up high")
        y_start(n, "below")
        y_arrived(n, "down low")
        y_start(n, "above")
        y_arrived(n, "on low", "on high")
        y_start(n, "far")

    def finish(n):
        y_arrived(n, "own", "below", "above", "far")

    def out_copy(f1):
        return pltpu.make_async_copy(staged.at[f1], out_hbm.at[f1], out_sem.at[f1])

    def last_copy(half):
        n = half * RADIX + RADIX - 1
        return pltpu.make_async_copy(gbufs[n], last_ref.at[half], out_sem.at[n])

    def make_tiles(f1):
        halves = [gbufs[half * RADIX + f1] for half in range(HALVES)]

        @pl.loop(0, 8, step=2)
        def _(first):
            for more in range(2):
                j = first + more
                blocks = [
                    jnp.concatenate([half[:, j, :, block * BLOCK : (block + 1) * BLOCK] for half in halves], axis=0)
                    for block in range(4)
                ]
                for slot in range(slots):
                    left, right = [sum(w * x for w, x in zip(side, blocks)) for side in weights[slot]]
                    total = correlate(left, right)
                    staged[f1, slot, j, 0] = total[:, :BLOCK]
                    staged[f1, slot, j, 1] = total[:, BLOCK:]

        out_copy(f1).start()

    history = pltpu.make_async_remote_copy(
        src_ref=v_hbm.at[:, pl.ds(0, 3)],
        dst_ref=v.at[:, pl.ds(8, 3)],
        send_sem=hist_sem.at[0],
        recv_sem=hist_sem.at[1],
        device_id=(c, previous),
        device_id_type=MESH,
    )

    def prepare(n):
        if n == half_chunks:
            history.wait_recv()

            @pl.when(t == tiles - 1)
            def _():
                for ri in range(2):
                    for frame in range(8, 11):
                        v[ri, frame] = jnp.zeros(v.shape[2:], jnp.float32)

            filter_half(1)
        transform(n)
        if n == 0:
            pl.semaphore_wait(barrier, chans - 1 + 4)
            history.start()
        turn_start(n)

    half_chunks = chunks // HALVES
    load_v.wait()
    load_taps.wait()
    filter_half(0)
    load_tab.wait()
    for n in range(AHEAD):
        prepare(n)
    for n in range(chunks + 3):
        if n < chunks:
            relay(n)
            start_own(n)
        if 0 <= n - 1 < chunks:
            start_near(n - 1)
        if n + AHEAD < chunks:
            prepare(n + AHEAD)
        if 0 <= n - 2 < chunks:
            start_far(n - 2)
        done = n - 3
        if 0 <= done < chunks:
            finish(done)
            half, f1 = done // RADIX, done % RADIX
            if f1 == RADIX - 1:
                last_copy(half).start()
            elif half == HALVES - 1:
                make_tiles(f1)
    history.wait_send()
    for n in range(chunks):
        turn_wait(n, turn_send)
        for copy in all_copies[n].values():
            copy.wait_send()
    for f1 in range(RADIX - 1):
        out_copy(f1).wait()
    for half in range(HALVES):
        last_copy(half).wait()


def in_hbm(*arrays):
    return [pltpu.with_memory_space_constraint(array, pltpu.HBM) for array in arrays]


def early_tiles(voltage, fir_taps, tables, tile_slot, tile_blocks, chans, tiles, slots):
    frames, inputs, samples = voltage.shape[1:]
    chunks = HALVES * RADIX
    f32 = jnp.float32
    any_space = pl.BlockSpec(memory_space=pl.ANY)
    smem = pl.BlockSpec(memory_space=pltpu.SMEM)
    return pl.pallas_call(
        functools.partial(turn_kernel, chans, tiles, slots),
        out_shape=(
            jax.ShapeDtypeStruct((RADIX - 1, slots, 8, 2, BLOCK, BLOCK), f32),
            jax.ShapeDtypeStruct((HALVES, tiles, 8, 8, 512), f32),
        ),
        in_specs=[any_space, any_space, any_space, smem, smem],
        out_specs=(any_space, any_space),
        scratch_shapes=[
            pltpu.VMEM((2, frames + 3, inputs, samples), f32),
            pltpu.VMEM(fir_taps.shape, f32),
            pltpu.VMEM(tables.shape, jnp.bfloat16),
            pltpu.VMEM((RADIX, 128, 512), jnp.bfloat16),
            pltpu.VMEM((RADIX, 128, 512), jnp.bfloat16),
            pltpu.VMEM((chunks, 256, 128), f32),
            pltpu.VMEM((chunks, 256, 128), f32),
            pltpu.VMEM((RADIX - 1, slots, 8, 2, BLOCK, BLOCK), f32),
            *[pltpu.VMEM((tiles, 8, 8, 512), f32) for _ in range(chunks)],
            pltpu.SemaphoreType.DMA((3,)),
            pltpu.SemaphoreType.DMA((2,)),
            pltpu.SemaphoreType.DMA((chunks,)),
            pltpu.SemaphoreType.DMA((chunks,)),
            pltpu.SemaphoreType.DMA((chunks, 10)),
            pltpu.SemaphoreType.DMA((chunks, 10)),
            pltpu.SemaphoreType.DMA((chunks,)),
        ],
        compiler_params=pltpu.CompilerParams(collective_id=0, has_side_effects=True, vmem_limit_bytes=TURN_LIMIT),
        name="turn",
    )(*in_hbm(voltage, fir_taps, tables, tile_slot, tile_blocks))


def tile_kernel(slot_ref, blocks_ref, early_ref, spectra_ref, out_hbm, staged, out_sem):
    t = lax.axis_index("tile")
    slots, step = staged.shape[:2]
    parts = [(f1, slot) for f1 in range(RADIX - 1) for slot in range(slots)]
    copies = []
    for i, (f1, slot) in enumerate(parts):
        copies.append(pltpu.make_async_copy(early_ref.at[f1, slot], out_hbm.at[slot, :, f1], out_sem.at[i]))
        copies[-1].start()
    halves = [spectra_ref.at[half] for half in range(HALVES)]
    for slot in range(slots):
        found, rows, cols = find_tile(slot_ref, blocks_ref, t * slots + slot)

        @pl.when(found > 0)
        def _():
            for j in range(step):
                left, right = [
                    jnp.concatenate([half[:, j, :, lanes] for half in halves], axis=0) for lanes in (rows, cols)
                ]
                total = correlate(left, right)
                staged[slot, j, 0] = total[:, :BLOCK]
                staged[slot, j, 1] = total[:, BLOCK:]

        @pl.when(found == 0)
        def _():
            staged[slot] = jnp.zeros(staged.shape[1:], jnp.float32)

        copies.append(
            pltpu.make_async_copy(staged.at[slot], out_hbm.at[slot, :, RADIX - 1], out_sem.at[len(parts) + slot])
        )
        copies[-1].start()
    for copy in copies:
        copy.wait()


def last_tiles(early, spectra, tile_slot, tile_blocks):
    slots = early.shape[1]
    smem = pl.BlockSpec(memory_space=pltpu.SMEM)
    any_space = pl.BlockSpec(memory_space=pl.ANY)
    return pl.pallas_call(
        tile_kernel,
        out_shape=jax.ShapeDtypeStruct((slots, 8, RADIX, 2, BLOCK, BLOCK), jnp.float32),
        in_specs=[smem, smem, any_space, pl.BlockSpec(memory_space=pltpu.VMEM)],
        out_specs=any_space,
        scratch_shapes=[
            pltpu.VMEM((slots, 8, 2, BLOCK, BLOCK), jnp.float32),
            pltpu.SemaphoreType.DMA((RADIX * slots,)),
        ],
        compiler_params=pltpu.CompilerParams(vmem_limit_bytes=LAST_LIMIT),
        name="tiles",
    )(*in_hbm(tile_slot, tile_blocks), early, spectra)


def solution(mesh):
    chans, tiles = mesh.shape["chan"], mesh.shape["tile"]

    def body(voltage, fir_taps, tile_slot, tile_blocks):
        channels = voltage.shape[3]
        spectra_total = voltage.shape[1] * tiles
        slots = -(-tile_slot.shape[0] // tiles)
        blocks = tile_blocks.T
        tables = jnp.asarray(dft_tables(channels, 1.0 / math.sqrt(channels * spectra_total)))
        early, last = early_tiles(voltage, fir_taps, tables, tile_slot, blocks, chans, tiles, slots)
        out = last_tiles(early, last, tile_slot, blocks)
        return out.reshape(slots, 8 * RADIX, 2, BLOCK, BLOCK)

    in_specs = (P(None, "tile", "chan", None), P(), P(), P())
    out_specs = P("tile", "chan", None, None, None)
    return jax.shard_map(body, mesh=mesh, in_specs=in_specs, out_specs=out_specs, check_vma=False)
```

```python
import functools
import math

import jax
import jax.numpy as jnp
import ml_dtypes
import numpy as np
from jax import lax
from jax.experimental import pallas as pl
from jax.experimental.pallas import tpu as pltpu
from jax.sharding import PartitionSpec as P

MESH = pl.DeviceIdType.MESH
BLOCK = 128
RADIX = 4
TURN_LIMIT = 40 << 20
LAST_LIMIT = 40 << 20
HALVES = 2
SPREAD = 3
AHEAD = 3


def dft_tables(channels, scale):
    inner = channels // RADIX
    k2 = np.arange(inner)
    f2 = np.arange(inner)
    tables = []
    for f1 in range(RADIX):
        phase = (k2[None, :] * (RADIX * f2[:, None] + f1)) % channels * (2.0 * math.pi / channels)
        both = np.concatenate([np.cos(phase), np.sin(phase)], axis=1) * scale
        head = both.astype(ml_dtypes.bfloat16)
        tail = (both - head.astype(np.float64)).astype(ml_dtypes.bfloat16)
        tables.append(np.stack([head, tail]))
    return np.stack(tables)


def head_tail(value):
    head = value.astype(jnp.bfloat16)
    return head, (value - head.astype(jnp.float32)).astype(jnp.bfloat16)


def turn_lanes(value):
    row = lax.broadcasted_iota(jnp.int32, value.shape, 0)
    lane = lax.broadcasted_iota(jnp.int32, value.shape, 1) // 16
    for bit in range(3):
        step = 1 << bit
        row_bit = (row // step) % 2
        lane_bit = (lane // step) % 2
        up = pltpu.roll(pltpu.roll(value, 16 * step, 1), 8 - step, 0)
        if bit == 2:
            down = up
        else:
            down = pltpu.roll(pltpu.roll(value, 128 - 16 * step, 1), step, 0)
        value = jnp.where(row_bit == lane_bit, value, jnp.where(row_bit == 0, up, down))
    return value


def find_tile(slot_ref, blocks_ref, wanted):
    found = jnp.int32(0)
    row_block = jnp.int32(0)
    col_block = jnp.int32(0)
    for r in range(slot_ref.shape[0]):
        hit = (slot_ref[r] == wanted).astype(jnp.int32)
        found += hit
        row_block += hit * blocks_ref[0, r]
        col_block += hit * blocks_ref[1, r]
    rows = pl.ds(pl.multiple_of(row_block * BLOCK, BLOCK), BLOCK)
    cols = pl.ds(pl.multiple_of(col_block * BLOCK, BLOCK), BLOCK)
    return found, rows, cols


def pick_weights(slot_ref, blocks_ref, wanted, side, blocks):
    weights = [jnp.float32(0)] * blocks
    for r in range(slot_ref.shape[0]):
        hit = slot_ref[r] == wanted
        for block in range(blocks):
            weights[block] += jnp.where(hit & (blocks_ref[side, r] == block), 1.0, 0.0)
    return weights


def correlate(left, right):
    sign = jnp.where(lax.broadcasted_iota(jnp.int32, (16, 8, BLOCK), 1) < 4, -1.0, 1.0)
    left = left.reshape(BLOCK, BLOCK)
    other = (pltpu.roll(right, 4, 1) * sign).reshape(BLOCK, BLOCK)
    both = jnp.concatenate([right.reshape(BLOCK, BLOCK), other], axis=1)
    left_head, left_tail = head_tail(left.T)
    both_head, both_tail = head_tail(both)
    dot = functools.partial(jnp.dot, preferred_element_type=jnp.float32)
    return dot(left_tail, both_head) + dot(left_head, both_tail) + dot(left_head, both_head)


def turn_kernel(
    chans, tiles, slots, v_hbm, taps_hbm, tab_hbm, slot_ref, blocks_ref, out_hbm, last_ref,
    v, taps_ref, tab, u_head, u_tail, sbuf, rbuf, bsend, brecv, staged, *rest,
):
    gbufs = rest[: HALVES * RADIX]
    load_sem, hist_sem, turn_send, turn_recv, y_send, y_recv, out_sem = rest[HALVES * RADIX :]
    c = lax.axis_index("chan")
    t = lax.axis_index("tile")
    chunks = sbuf.shape[0]

    barrier = pltpu.get_barrier_semaphore()

    @pl.loop(1, chans)
    def _(i):
        pl.semaphore_signal(barrier, inc=1, device_id=(lax.rem(c + i, chans), t), device_id_type=MESH)

    for step in (1, 2, tiles - 1, tiles - 2):
        pl.semaphore_signal(barrier, inc=1, device_id=(c, lax.rem(t + step, tiles)), device_id_type=MESH)

    up = lax.rem(t + 2, tiles)
    down = lax.rem(t + tiles - 2, tiles)
    far = lax.rem(t + 4, tiles)
    partner = t + 1 - 2 * lax.rem(t, 2)
    previous = lax.rem(t + tiles - 1, tiles)

    load_v = pltpu.make_async_copy(v_hbm, v.at[:, pl.ds(0, 8)], load_sem.at[0])
    load_tab = pltpu.make_async_copy(tab_hbm, tab, load_sem.at[1])
    load_taps = pltpu.make_async_copy(taps_hbm, taps_ref, load_sem.at[2])
    load_v.start()
    load_taps.start()
    load_tab.start()

    def filter_half(half):
        @pl.loop(0, 4)
        def _(s):
            for kb in range(2):
                part = []
                for k1 in range(RADIX):
                    lanes = pl.ds(k1 * 256 + kb * 128, 128)
                    for ri in range(2):
                        total = jnp.zeros((16, 128), jnp.float32)
                        for tap in range(4):
                            total = total + taps_ref[pl.ds(tap, 1), lanes] * v[ri, half * 4 + s + tap, :, lanes]
                        part.append(total)
                r = part[0::2]
                m = part[1::2]
                sum_r, sum_m = r[0] + r[2], m[0] + m[2]
                dif_r, dif_m = r[0] - r[2], m[0] - m[2]
                odd_r, odd_m = r[1] + r[3], m[1] + m[3]
                odf_r, odf_m = r[1] - r[3], m[1] - m[3]
                turned = (
                    (sum_r + odd_r, sum_m + odd_m),
                    (dif_r + odf_m, dif_m - odf_r),
                    (sum_r - odd_r, sum_m - odd_m),
                    (dif_r - odf_m, dif_m + odf_r),
                )
                row = pl.multiple_of(s * 16, 16)
                for f1 in range(RADIX):
                    re, im = turned[f1]
                    re_h, re_t = head_tail(re)
                    im_h, im_t = head_tail(im)
                    first = pl.ds(kb * 128, 128)
                    second = pl.ds(256 + kb * 128, 128)
                    u_head[f1, pl.ds(row, 16), first] = re_h
                    u_tail[f1, pl.ds(row, 16), first] = re_t
                    u_head[f1, pl.ds(row, 16), second] = im_h
                    u_tail[f1, pl.ds(row, 16), second] = im_t
                    u_head[f1, pl.ds(64 + row, 16), first] = im_h
                    u_tail[f1, pl.ds(64 + row, 16), first] = im_t
                    u_head[f1, pl.ds(64 + row, 16), second] = -re_h
                    u_tail[f1, pl.ds(64 + row, 16), second] = -re_t

    def transform(n):
        f1 = n % RADIX
        dims = (((1,), (1,)), ((), ()))
        dot = functools.partial(lax.dot_general, dimension_numbers=dims, preferred_element_type=jnp.float32)
        head, tail = u_head[f1], u_tail[f1]
        spectra = dot(tab[f1, 0], tail) + dot(tab[f1, 1], head) + dot(tab[f1, 0], head)
        if n == SPREAD:
            bsend[lax.div(t, 2)] = spectra
        else:
            sbuf[n] = spectra

    def turn_copy(source, target, sem, to):
        return pltpu.make_async_remote_copy(
            src_ref=source.at[pl.ds(pl.multiple_of(to * 8, 8), 8)],
            dst_ref=target.at[pl.ds(pl.multiple_of(c * 8, 8), 8)],
            send_sem=turn_send.at[sem],
            recv_sem=turn_recv.at[sem],
            device_id=(to, t),
            device_id_type=MESH,
        )

    def turn_start(source, target, sem):
        turn_copy(source, target, sem, lax.rem(c + chans // 2, chans)).start()

        @pl.loop(1, chans // 2)
        def _(i):
            turn_copy(source, target, sem, lax.rem(c + i, chans)).start()
            turn_copy(source, target, sem, lax.rem(c + chans - i, chans)).start()

    def turn_wait(source, target, sems, sem):
        rows = pl.ds(0, (chans - 1) * 8)
        pltpu.make_async_copy(source.at[rows], target.at[rows], sems.at[sem]).wait()

    def relay(source, target, sem, n, block):
        turn_wait(source, target, turn_recv, sem)
        mine = pl.ds(pl.multiple_of(c * 8, 8), 8)
        target[mine] = source[mine]
        for j in range(8):
            for a in range(4):
                gbufs[n][block, j, :, pl.ds(a * 128, 128)] = turn_lanes(target[pl.ds(64 * a + j, 8, stride=8), :])

    def y_copy(n, block, to, slot, part=pl.ds(0, 8)):
        where = gbufs[n].at[block, part]
        return pltpu.make_async_remote_copy(
            src_ref=where,
            dst_ref=where,
            send_sem=y_send.at[n, slot],
            recv_sem=y_recv.at[n, slot],
            device_id=(c, to),
            device_id_type=MESH,
        )

    low, high = pl.ds(0, 4), pl.ds(4, 4)

    def y_copies(n):
        return {
            "up low": y_copy(n, t, up, 0, low),
            "down high": y_copy(n, t, down, 1, high),
            "up high": y_copy(n, t, up, 2, high),
            "down low": y_copy(n, t, down, 3, low),
            "own": y_copy(n, t, partner, 4),
            "on low": y_copy(n, down, up, 5, low),
            "on high": y_copy(n, up, down, 6, high),
            "below": y_copy(n, down, partner, 7),
            "above": y_copy(n, up, partner, 8),
            "far": y_copy(n, far, partner, 9),
        }

    all_copies = [y_copies(n) for n in range(chunks)]

    def spread_copy(block, to, slot, part):
        where = bsend.at[lax.div(block, 2), part]
        return pltpu.make_async_remote_copy(
            src_ref=where,
            dst_ref=where,
            send_sem=y_send.at[SPREAD, slot],
            recv_sem=y_recv.at[SPREAD, slot],
            device_id=(c, to),
            device_id_type=MESH,
        )

    first, second = pl.ds(0, 4 * chans), pl.ds(4 * chans, 4 * chans)
    all_copies[SPREAD].update({
        "up low": spread_copy(t, up, 0, first),
        "down high": spread_copy(t, down, 1, second),
        "up high": spread_copy(t, up, 2, second),
        "down low": spread_copy(t, down, 3, first),
        "on low": spread_copy(down, up, 5, first),
        "on high": spread_copy(up, down, 6, second),
    })
    spread_blocks = [(t, "own"), (down, "below"), (up, "above"), (far, "far")]

    def spread_refs(i):
        index = lax.div(spread_blocks[i][0], 2)
        return bsend.at[index], brecv.at[index], chunks + i

    def spread_start(i):
        if i == 1:
            y_arrived(SPREAD, "up high")
        elif i == 2:
            y_arrived(SPREAD, "down low")
        elif i == 3:
            y_arrived(SPREAD, "on low", "on high")
        turn_start(*spread_refs(i))

    def spread_relay(i):
        relay(*spread_refs(i), SPREAD, spread_blocks[i][0])
        y_start(SPREAD, spread_blocks[i][1])

    def chunk_refs(n):
        return sbuf.at[n], rbuf.at[n], n

    def y_start(n, *names):
        for name in names:
            all_copies[n][name].start()

    def y_arrived(n, *names):
        for name in names:
            all_copies[n][name].wait_recv()

    def start_own(n):
        y_start(n, "up low", "down high", "up high", "down low", "own")

    def start_near(n):
        y_arrived(n, "up low")
        y_start(n, "on low")
        y_arrived(n, "down high")
        y_start(n, "on high")

    def start_far(n):
        y_arrived(n, "up high")
        y_start(n, "below")
        y_arrived(n, "down low")
        y_start(n, "above")
        y_arrived(n, "on low", "on high")
        y_start(n, "far")

    def finish(n):
        y_arrived(n, "own", "below", "above", "far")

    def out_copy(f1):
        return pltpu.make_async_copy(staged.at[f1], out_hbm.at[f1], out_sem.at[f1])

    def last_copy(half):
        n = half * RADIX + RADIX - 1
        return pltpu.make_async_copy(gbufs[n], last_ref.at[half], out_sem.at[n])

    def make_tiles(f1, weights):
        halves = [gbufs[half * RADIX + f1] for half in range(HALVES)]

        @pl.loop(0, 8, step=2)
        def _(first):
            for more in range(2):
                j = first + more
                blocks = [
                    jnp.concatenate([half[:, j, :, block * BLOCK : (block + 1) * BLOCK] for half in halves], axis=0)
                    for block in range(4)
                ]
                for slot in range(slots):
                    left, right = [sum(w * x for w, x in zip(side, blocks)) for side in weights[slot]]
                    total = correlate(left, right)
                    staged[f1, slot, j, 0] = total[:, :BLOCK]
                    staged[f1, slot, j, 1] = total[:, BLOCK:]

        out_copy(f1).start()

    history = pltpu.make_async_remote_copy(
        src_ref=v_hbm.at[:, pl.ds(0, 3)],
        dst_ref=v.at[:, pl.ds(8, 3)],
        send_sem=hist_sem.at[0],
        recv_sem=hist_sem.at[1],
        device_id=(c, previous),
        device_id_type=MESH,
    )

    half_chunks = chunks // HALVES

    def prepare(n):
        if n == half_chunks:
            history.wait_recv()

            @pl.when(t == tiles - 1)
            def _():
                for ri in range(2):
                    for frame in range(8, 11):
                        v[ri, frame] = jnp.zeros(v.shape[2:], jnp.float32)

            filter_half(1)
        transform(n)
        turn_start(*chunk_refs(n))

    load_v.wait()
    load_taps.wait()
    filter_half(0)
    load_tab.wait()
    transform(SPREAD)
    pl.semaphore_wait(barrier, chans - 1 + 4)
    y_start(SPREAD, "up low", "down high", "up high", "down low")
    history.start()
    normal = [n for n in range(chunks) if n != SPREAD]
    for n in normal[:AHEAD]:
        prepare(n)
    weights = [
        [pick_weights(slot_ref, blocks_ref, t * slots + slot, side, 4) for side in range(2)] for slot in range(slots)
    ]

    for step in range(len(normal) + 3):
        if step < len(normal):
            n = normal[step]
            relay(*chunk_refs(n), n, t)
            start_own(n)
        if step == 0:
            start_near(SPREAD)
            spread_start(0)
        if 0 <= step - 1 < len(normal):
            start_near(normal[step - 1])
        if step + AHEAD < len(normal):
            prepare(normal[step + AHEAD])
        if 1 <= step < 4:
            spread_start(step)
        if 0 <= step - 4 < 4:
            spread_relay(step - 4)
        if 0 <= step - 2 < len(normal):
            start_far(normal[step - 2])
        if 0 <= step - 3 < len(normal):
            n = normal[step - 3]
            finish(n)
            half, f1 = n // RADIX, n % RADIX
            if f1 == RADIX - 1:
                finish(SPREAD)
                last_copy(0).start()
                last_copy(1).start()
            elif half == HALVES - 1:
                make_tiles(f1, weights)
    history.wait_send()
    for n in normal:
        turn_wait(sbuf.at[n], rbuf.at[n], turn_send, n)
    for i in range(4):
        turn_wait(bsend.at[0], brecv.at[0], turn_send, chunks + i)
    for n in range(chunks):
        for copy in all_copies[n].values():
            copy.wait_send()
    for f1 in range(RADIX - 1):
        out_copy(f1).wait()
    for half in range(HALVES):
        last_copy(half).wait()


def in_hbm(*arrays):
    return [pltpu.with_memory_space_constraint(array, pltpu.HBM) for array in arrays]


def early_tiles(voltage, fir_taps, tables, tile_slot, tile_blocks, chans, tiles, slots):
    frames, inputs, samples = voltage.shape[1:]
    chunks = HALVES * RADIX
    f32 = jnp.float32
    any_space = pl.BlockSpec(memory_space=pl.ANY)
    smem = pl.BlockSpec(memory_space=pltpu.SMEM)
    return pl.pallas_call(
        functools.partial(turn_kernel, chans, tiles, slots),
        out_shape=(
            jax.ShapeDtypeStruct((RADIX - 1, slots, 8, 2, BLOCK, BLOCK), f32),
            jax.ShapeDtypeStruct((HALVES, tiles, 8, 8, 512), f32),
        ),
        in_specs=[any_space, any_space, any_space, smem, smem],
        out_specs=(any_space, any_space),
        scratch_shapes=[
            pltpu.VMEM((2, frames + 3, inputs, samples), f32),
            pltpu.VMEM(fir_taps.shape, f32),
            pltpu.VMEM(tables.shape, jnp.bfloat16),
            pltpu.VMEM((RADIX, 128, 512), jnp.bfloat16),
            pltpu.VMEM((RADIX, 128, 512), jnp.bfloat16),
            pltpu.VMEM((chunks, 256, 128), f32),
            pltpu.VMEM((chunks, 256, 128), f32),
            pltpu.VMEM((tiles // 2, 256, 128), f32),
            pltpu.VMEM((tiles // 2, 256, 128), f32),
            pltpu.VMEM((RADIX - 1, slots, 8, 2, BLOCK, BLOCK), f32),
            *[pltpu.VMEM((tiles, 8, 8, 512), f32) for _ in range(chunks)],
            pltpu.SemaphoreType.DMA((3,)),
            pltpu.SemaphoreType.DMA((2,)),
            pltpu.SemaphoreType.DMA((chunks + 4,)),
            pltpu.SemaphoreType.DMA((chunks + 4,)),
            pltpu.SemaphoreType.DMA((chunks, 10)),
            pltpu.SemaphoreType.DMA((chunks, 10)),
            pltpu.SemaphoreType.DMA((chunks,)),
        ],
        compiler_params=pltpu.CompilerParams(collective_id=0, has_side_effects=True, vmem_limit_bytes=TURN_LIMIT),
        name="turn",
    )(*in_hbm(voltage, fir_taps, tables, tile_slot, tile_blocks))


def tile_kernel(slot_ref, blocks_ref, early_ref, spectra_ref, out_hbm, staged, out_sem):
    t = lax.axis_index("tile")
    slots, step = staged.shape[:2]
    parts = [(f1, slot) for f1 in range(RADIX - 1) for slot in range(slots)]
    copies = []
    for i, (f1, slot) in enumerate(parts):
        copies.append(pltpu.make_async_copy(early_ref.at[f1, slot], out_hbm.at[slot, :, f1], out_sem.at[i]))
        copies[-1].start()
    halves = [spectra_ref.at[half] for half in range(HALVES)]
    for slot in range(slots):
        found, rows, cols = find_tile(slot_ref, blocks_ref, t * slots + slot)

        @pl.when(found > 0)
        def _():
            for j in range(step):
                left, right = [
                    jnp.concatenate([half[:, j, :, lanes] for half in halves], axis=0) for lanes in (rows, cols)
                ]
                total = correlate(left, right)
                staged[slot, j, 0] = total[:, :BLOCK]
                staged[slot, j, 1] = total[:, BLOCK:]

        @pl.when(found == 0)
        def _():
            staged[slot] = jnp.zeros(staged.shape[1:], jnp.float32)

        copies.append(
            pltpu.make_async_copy(staged.at[slot], out_hbm.at[slot, :, RADIX - 1], out_sem.at[len(parts) + slot])
        )
        copies[-1].start()
    for copy in copies:
        copy.wait()


def last_tiles(early, spectra, tile_slot, tile_blocks):
    slots = early.shape[1]
    smem = pl.BlockSpec(memory_space=pltpu.SMEM)
    any_space = pl.BlockSpec(memory_space=pl.ANY)
    return pl.pallas_call(
        tile_kernel,
        out_shape=jax.ShapeDtypeStruct((slots, 8, RADIX, 2, BLOCK, BLOCK), jnp.float32),
        in_specs=[smem, smem, any_space, pl.BlockSpec(memory_space=pltpu.VMEM)],
        out_specs=any_space,
        scratch_shapes=[
            pltpu.VMEM((slots, 8, 2, BLOCK, BLOCK), jnp.float32),
            pltpu.SemaphoreType.DMA((RADIX * slots,)),
        ],
        compiler_params=pltpu.CompilerParams(vmem_limit_bytes=LAST_LIMIT),
        name="tiles",
    )(*in_hbm(tile_slot, tile_blocks), early, spectra)


def solution(mesh):
    chans, tiles = mesh.shape["chan"], mesh.shape["tile"]

    def body(voltage, fir_taps, tile_slot, tile_blocks):
        channels = voltage.shape[3]
        spectra_total = voltage.shape[1] * tiles
        slots = -(-tile_slot.shape[0] // tiles)
        blocks = tile_blocks.T
        tables = jnp.asarray(dft_tables(channels, 1.0 / math.sqrt(channels * spectra_total)))
        early, last = early_tiles(voltage, fir_taps, tables, tile_slot, blocks, chans, tiles, slots)
        out = last_tiles(early, last, tile_slot, blocks)
        return out.reshape(slots, 8 * RADIX, 2, BLOCK, BLOCK)

    in_specs = (P(None, "tile", "chan", None), P(), P(), P())
    out_specs = P("tile", "chan", None, None, None)
    return jax.shard_map(body, mesh=mesh, in_specs=in_specs, out_specs=out_specs, check_vma=False)
```

```python
import functools
import math

import jax
import jax.numpy as jnp
import ml_dtypes
import numpy as np
from jax import lax
from jax.experimental import pallas as pl
from jax.experimental.pallas import tpu as pltpu
from jax.sharding import PartitionSpec as P

MESH = pl.DeviceIdType.MESH
BLOCK = 128
RADIX = 4
TURN_LIMIT = 40 << 20
LAST_LIMIT = 40 << 20
HALVES = 2
SPREAD = 3
DEPTH_Z = 8
AHEAD = 3


def dft_tables(channels, scale):
    inner = channels // RADIX
    k2 = np.arange(inner)
    f2 = np.arange(inner)
    tables = []
    for f1 in range(RADIX):
        phase = (k2[None, :] * (RADIX * f2[:, None] + f1)) % channels * (2.0 * math.pi / channels)
        both = np.concatenate([np.cos(phase), np.sin(phase)], axis=1) * scale
        head = both.astype(ml_dtypes.bfloat16)
        tail = (both - head.astype(np.float64)).astype(ml_dtypes.bfloat16)
        tables.append(np.stack([head, tail]))
    return np.stack(tables)


def head_tail(value):
    head = value.astype(jnp.bfloat16)
    return head, (value - head.astype(jnp.float32)).astype(jnp.bfloat16)


def turn_lanes(value):
    row = lax.broadcasted_iota(jnp.int32, value.shape, 0)
    lane = lax.broadcasted_iota(jnp.int32, value.shape, 1) // 16
    for bit in range(3):
        step = 1 << bit
        row_bit = (row // step) % 2
        lane_bit = (lane // step) % 2
        up = pltpu.roll(pltpu.roll(value, 16 * step, 1), 8 - step, 0)
        if bit == 2:
            down = up
        else:
            down = pltpu.roll(pltpu.roll(value, 128 - 16 * step, 1), step, 0)
        value = jnp.where(row_bit == lane_bit, value, jnp.where(row_bit == 0, up, down))
    return value


def find_tile(slot_ref, blocks_ref, wanted):
    found = jnp.int32(0)
    row_block = jnp.int32(0)
    col_block = jnp.int32(0)
    for r in range(slot_ref.shape[0]):
        hit = (slot_ref[r] == wanted).astype(jnp.int32)
        found += hit
        row_block += hit * blocks_ref[0, r]
        col_block += hit * blocks_ref[1, r]
    rows = pl.ds(pl.multiple_of(row_block * BLOCK, BLOCK), BLOCK)
    cols = pl.ds(pl.multiple_of(col_block * BLOCK, BLOCK), BLOCK)
    return found, rows, cols


def pick_weights(slot_ref, blocks_ref, wanted, side, blocks):
    weights = [jnp.float32(0)] * blocks
    for r in range(slot_ref.shape[0]):
        hit = slot_ref[r] == wanted
        for block in range(blocks):
            weights[block] += jnp.where(hit & (blocks_ref[side, r] == block), 1.0, 0.0)
    return weights


def correlate(left, right):
    sign = jnp.where(lax.broadcasted_iota(jnp.int32, (16, 8, BLOCK), 1) < 4, -1.0, 1.0)
    left = left.reshape(BLOCK, BLOCK)
    other = (pltpu.roll(right, 4, 1) * sign).reshape(BLOCK, BLOCK)
    both = jnp.concatenate([right.reshape(BLOCK, BLOCK), other], axis=1)
    left_head, left_tail = head_tail(left.T)
    both_head, both_tail = head_tail(both)
    dot = functools.partial(jnp.dot, preferred_element_type=jnp.float32)
    return dot(left_tail, both_head) + dot(left_head, both_tail) + dot(left_head, both_head)


def turn_kernel(
    chans, tiles, slots, v_hbm, taps_hbm, tab_hbm, slot_ref, blocks_ref, out_hbm, last_ref,
    v, taps_ref, tab, u_head, u_tail, sbuf, rbuf, bsend, brecv, staged, *rest,
):
    gbufs = rest[: HALVES * RADIX]
    load_sem, hist_sem, turn_send, turn_recv, y_send, y_recv, out_sem = rest[HALVES * RADIX :]
    c = lax.axis_index("chan")
    t = lax.axis_index("tile")
    chunks = sbuf.shape[0]

    barrier = pltpu.get_barrier_semaphore()

    @pl.loop(1, chans)
    def _(i):
        pl.semaphore_signal(barrier, inc=1, device_id=(lax.rem(c + i, chans), t), device_id_type=MESH)

    for step in (1, 2, tiles - 1, tiles - 2):
        pl.semaphore_signal(barrier, inc=1, device_id=(c, lax.rem(t + step, tiles)), device_id_type=MESH)

    up = lax.rem(t + 2, tiles)
    down = lax.rem(t + tiles - 2, tiles)
    far = lax.rem(t + 4, tiles)
    partner = t + 1 - 2 * lax.rem(t, 2)
    previous = lax.rem(t + tiles - 1, tiles)

    load_v = pltpu.make_async_copy(v_hbm, v.at[:, pl.ds(0, 8)], load_sem.at[0])
    load_tab = pltpu.make_async_copy(tab_hbm, tab, load_sem.at[1])
    load_taps = pltpu.make_async_copy(taps_hbm, taps_ref, load_sem.at[2])
    load_v.start()
    load_taps.start()
    load_tab.start()

    def filter_half(half):
        @pl.loop(0, 4)
        def _(s):
            for kb in range(2):
                part = []
                for k1 in range(RADIX):
                    lanes = pl.ds(k1 * 256 + kb * 128, 128)
                    for ri in range(2):
                        total = jnp.zeros((16, 128), jnp.float32)
                        for tap in range(4):
                            total = total + taps_ref[pl.ds(tap, 1), lanes] * v[ri, half * 4 + s + tap, :, lanes]
                        part.append(total)
                r = part[0::2]
                m = part[1::2]
                sum_r, sum_m = r[0] + r[2], m[0] + m[2]
                dif_r, dif_m = r[0] - r[2], m[0] - m[2]
                odd_r, odd_m = r[1] + r[3], m[1] + m[3]
                odf_r, odf_m = r[1] - r[3], m[1] - m[3]
                turned = (
                    (sum_r + odd_r, sum_m + odd_m),
                    (dif_r + odf_m, dif_m - odf_r),
                    (sum_r - odd_r, sum_m - odd_m),
                    (dif_r - odf_m, dif_m + odf_r),
                )
                row = pl.multiple_of(s * 16, 16)
                for f1 in range(RADIX):
                    re, im = turned[f1]
                    re_h, re_t = head_tail(re)
                    im_h, im_t = head_tail(im)
                    first = pl.ds(kb * 128, 128)
                    second = pl.ds(256 + kb * 128, 128)
                    u_head[f1, pl.ds(row, 16), first] = re_h
                    u_tail[f1, pl.ds(row, 16), first] = re_t
                    u_head[f1, pl.ds(row, 16), second] = im_h
                    u_tail[f1, pl.ds(row, 16), second] = im_t
                    u_head[f1, pl.ds(64 + row, 16), first] = im_h
                    u_tail[f1, pl.ds(64 + row, 16), first] = im_t
                    u_head[f1, pl.ds(64 + row, 16), second] = -re_h
                    u_tail[f1, pl.ds(64 + row, 16), second] = -re_t

    def transform(n):
        f1 = n % RADIX
        dims = (((1,), (1,)), ((), ()))
        dot = functools.partial(lax.dot_general, dimension_numbers=dims, preferred_element_type=jnp.float32)
        head, tail = u_head[f1], u_tail[f1]
        spectra = dot(tab[f1, 0], tail) + dot(tab[f1, 1], head) + dot(tab[f1, 0], head)
        if n == SPREAD:
            bsend[lax.div(t, 2)] = spectra
        else:
            sbuf[n] = spectra

    def peer(across, along):
        line = lax.rem(lax.div(c, DEPTH_Z) + across, chans // DEPTH_Z)
        return line * DEPTH_Z + lax.rem(lax.rem(c, DEPTH_Z) + along, DEPTH_Z)

    def turn_copy(source, target, sem, to):
        return pltpu.make_async_remote_copy(
            src_ref=source.at[pl.ds(pl.multiple_of(to * 8, 8), 8)],
            dst_ref=target.at[pl.ds(pl.multiple_of(c * 8, 8), 8)],
            send_sem=turn_send.at[sem],
            recv_sem=turn_recv.at[sem],
            device_id=(to, t),
            device_id_type=MESH,
        )

    def turn_start(source, target, sem):
        @pl.loop(0, DEPTH_Z - 1)
        def _(k):
            half = lax.div(k + 1, 2)
            along = DEPTH_Z // 2 + half - 2 * half * lax.rem(k, 2)
            for across in (2, 1, 3, 0):
                turn_copy(source, target, sem, peer(across, along)).start()

        for across in (2, 1, 3):
            turn_copy(source, target, sem, peer(across, 0)).start()

    def turn_wait(source, target, sems, sem):
        rows = pl.ds(0, (chans - 1) * 8)
        pltpu.make_async_copy(source.at[rows], target.at[rows], sems.at[sem]).wait()

    def relay(source, target, sem, n, block):
        turn_wait(source, target, turn_recv, sem)
        mine = pl.ds(pl.multiple_of(c * 8, 8), 8)
        target[mine] = source[mine]
        for j in range(8):
            for a in range(4):
                gbufs[n][block, j, :, pl.ds(a * 128, 128)] = turn_lanes(target[pl.ds(64 * a + j, 8, stride=8), :])

    def y_copy(n, block, to, slot, part=pl.ds(0, 8)):
        where = gbufs[n].at[block, part]
        return pltpu.make_async_remote_copy(
            src_ref=where,
            dst_ref=where,
            send_sem=y_send.at[n, slot],
            recv_sem=y_recv.at[n, slot],
            device_id=(c, to),
            device_id_type=MESH,
        )

    low, high = pl.ds(0, 4), pl.ds(4, 4)

    def y_copies(n):
        return {
            "up low": y_copy(n, t, up, 0, low),
            "down high": y_copy(n, t, down, 1, high),
            "up high": y_copy(n, t, up, 2, high),
            "down low": y_copy(n, t, down, 3, low),
            "own": y_copy(n, t, partner, 4),
            "on low": y_copy(n, down, up, 5, low),
            "on high": y_copy(n, up, down, 6, high),
            "below": y_copy(n, down, partner, 7),
            "above": y_copy(n, up, partner, 8),
            "far": y_copy(n, far, partner, 9),
        }

    all_copies = [y_copies(n) for n in range(chunks)]

    def spread_copy(block, to, slot, part):
        where = bsend.at[lax.div(block, 2), part]
        return pltpu.make_async_remote_copy(
            src_ref=where,
            dst_ref=where,
            send_sem=y_send.at[SPREAD, slot],
            recv_sem=y_recv.at[SPREAD, slot],
            device_id=(c, to),
            device_id_type=MESH,
        )

    first, second = pl.ds(0, 4 * chans), pl.ds(4 * chans, 4 * chans)
    all_copies[SPREAD].update({
        "up low": spread_copy(t, up, 0, first),
        "down high": spread_copy(t, down, 1, second),
        "up high": spread_copy(t, up, 2, second),
        "down low": spread_copy(t, down, 3, first),
        "on low": spread_copy(down, up, 5, first),
        "on high": spread_copy(up, down, 6, second),
    })
    spread_blocks = [(t, "own"), (down, "below"), (up, "above"), (far, "far")]

    def spread_refs(i):
        index = lax.div(spread_blocks[i][0], 2)
        return bsend.at[index], brecv.at[index], chunks + i

    def spread_start(i):
        if i == 1:
            y_arrived(SPREAD, "up high")
        elif i == 2:
            y_arrived(SPREAD, "down low")
        elif i == 3:
            y_arrived(SPREAD, "on low", "on high")
        turn_start(*spread_refs(i))

    def spread_relay(i):
        relay(*spread_refs(i), SPREAD, spread_blocks[i][0])
        y_start(SPREAD, spread_blocks[i][1])

    def chunk_refs(n):
        return sbuf.at[n], rbuf.at[n], n

    def y_start(n, *names):
        for name in names:
            all_copies[n][name].start()

    def y_arrived(n, *names):
        for name in names:
            all_copies[n][name].wait_recv()

    def start_own(n):
        y_start(n, "up low", "down high", "up high", "down low", "own")

    def start_near(n):
        y_arrived(n, "up low")
        y_start(n, "on low")
        y_arrived(n, "down high")
        y_start(n, "on high")

    def start_far(n):
        y_arrived(n, "up high")
        y_start(n, "below")
        y_arrived(n, "down low")
        y_start(n, "above")
        y_arrived(n, "on low", "on high")
        y_start(n, "far")

    def finish(n):
        y_arrived(n, "own", "below", "above", "far")

    def out_copy(f1):
        return pltpu.make_async_copy(staged.at[f1], out_hbm.at[f1], out_sem.at[f1])

    def last_copy(half):
        n = half * RADIX + RADIX - 1
        return pltpu.make_async_copy(gbufs[n], last_ref.at[half], out_sem.at[n])

    def make_tiles(f1, weights):
        halves = [gbufs[half * RADIX + f1] for half in range(HALVES)]

        @pl.loop(0, 8, step=2)
        def _(first):
            for more in range(2):
                j = first + more
                blocks = [
                    jnp.concatenate([half[:, j, :, block * BLOCK : (block + 1) * BLOCK] for half in halves], axis=0)
                    for block in range(4)
                ]
                for slot in range(slots):
                    left, right = [sum(w * x for w, x in zip(side, blocks)) for side in weights[slot]]
                    total = correlate(left, right)
                    staged[f1, slot, j, 0] = total[:, :BLOCK]
                    staged[f1, slot, j, 1] = total[:, BLOCK:]

        out_copy(f1).start()

    history = pltpu.make_async_remote_copy(
        src_ref=v_hbm.at[:, pl.ds(0, 3)],
        dst_ref=v.at[:, pl.ds(8, 3)],
        send_sem=hist_sem.at[0],
        recv_sem=hist_sem.at[1],
        device_id=(c, previous),
        device_id_type=MESH,
    )

    half_chunks = chunks // HALVES

    def prepare(n):
        if n == half_chunks:
            history.wait_recv()

            @pl.when(t == tiles - 1)
            def _():
                for ri in range(2):
                    for frame in range(8, 11):
                        v[ri, frame] = jnp.zeros(v.shape[2:], jnp.float32)

            filter_half(1)
        if n > 0:
            transform(n)
        turn_start(*chunk_refs(n))

    load_v.wait()
    load_taps.wait()
    filter_half(0)
    load_tab.wait()
    transform(SPREAD)
    transform(0)
    pl.semaphore_wait(barrier, chans - 1 + 4)
    normal = [n for n in range(chunks) if n != SPREAD]
    prepare(normal[0])
    y_start(SPREAD, "up low", "down high", "up high", "down low")
    history.start()
    for n in normal[1:AHEAD]:
        prepare(n)
    weights = [
        [pick_weights(slot_ref, blocks_ref, t * slots + slot, side, 4) for side in range(2)] for slot in range(slots)
    ]

    for step in range(len(normal) + 3):
        if step < len(normal):
            n = normal[step]
            relay(*chunk_refs(n), n, t)
            start_own(n)
        if step == 0:
            start_near(SPREAD)
            spread_start(0)
        if 0 <= step - 1 < len(normal):
            start_near(normal[step - 1])
        if step + AHEAD < len(normal):
            prepare(normal[step + AHEAD])
        if 1 <= step < 4:
            spread_start(step)
        if 0 <= step - 4 < 4:
            spread_relay(step - 4)
        if 0 <= step - 2 < len(normal):
            start_far(normal[step - 2])
        if 0 <= step - 3 < len(normal):
            n = normal[step - 3]
            finish(n)
            half, f1 = n // RADIX, n % RADIX
            if f1 == RADIX - 1:
                finish(SPREAD)
                last_copy(0).start()
                last_copy(1).start()
            elif half == HALVES - 1:
                make_tiles(f1, weights)
    history.wait_send()
    for n in normal:
        turn_wait(sbuf.at[n], rbuf.at[n], turn_send, n)
    for i in range(4):
        turn_wait(bsend.at[0], brecv.at[0], turn_send, chunks + i)
    for n in range(chunks):
        for copy in all_copies[n].values():
            copy.wait_send()
    for f1 in range(RADIX - 1):
        out_copy(f1).wait()
    for half in range(HALVES):
        last_copy(half).wait()


def in_hbm(*arrays):
    return [pltpu.with_memory_space_constraint(array, pltpu.HBM) for array in arrays]


def early_tiles(voltage, fir_taps, tables, tile_slot, tile_blocks, chans, tiles, slots):
    frames, inputs, samples = voltage.shape[1:]
    chunks = HALVES * RADIX
    f32 = jnp.float32
    any_space = pl.BlockSpec(memory_space=pl.ANY)
    smem = pl.BlockSpec(memory_space=pltpu.SMEM)
    return pl.pallas_call(
        functools.partial(turn_kernel, chans, tiles, slots),
        out_shape=(
            jax.ShapeDtypeStruct((RADIX - 1, slots, 8, 2, BLOCK, BLOCK), f32),
            jax.ShapeDtypeStruct((HALVES, tiles, 8, 8, 512), f32),
        ),
        in_specs=[any_space, any_space, any_space, smem, smem],
        out_specs=(any_space, any_space),
        scratch_shapes=[
            pltpu.VMEM((2, frames + 3, inputs, samples), f32),
            pltpu.VMEM(fir_taps.shape, f32),
            pltpu.VMEM(tables.shape, jnp.bfloat16),
            pltpu.VMEM((RADIX, 128, 512), jnp.bfloat16),
            pltpu.VMEM((RADIX, 128, 512), jnp.bfloat16),
            pltpu.VMEM((chunks, 256, 128), f32),
            pltpu.VMEM((chunks, 256, 128), f32),
            pltpu.VMEM((tiles // 2, 256, 128), f32),
            pltpu.VMEM((tiles // 2, 256, 128), f32),
            pltpu.VMEM((RADIX - 1, slots, 8, 2, BLOCK, BLOCK), f32),
            *[pltpu.VMEM((tiles, 8, 8, 512), f32) for _ in range(chunks)],
            pltpu.SemaphoreType.DMA((3,)),
            pltpu.SemaphoreType.DMA((2,)),
            pltpu.SemaphoreType.DMA((chunks + 4,)),
            pltpu.SemaphoreType.DMA((chunks + 4,)),
            pltpu.SemaphoreType.DMA((chunks, 10)),
            pltpu.SemaphoreType.DMA((chunks, 10)),
            pltpu.SemaphoreType.DMA((chunks,)),
        ],
        compiler_params=pltpu.CompilerParams(collective_id=0, has_side_effects=True, vmem_limit_bytes=TURN_LIMIT),
        name="turn",
    )(*in_hbm(voltage, fir_taps, tables, tile_slot, tile_blocks))


def tile_kernel(slot_ref, blocks_ref, early_ref, spectra_ref, out_hbm, staged, out_sem):
    t = lax.axis_index("tile")
    slots, step = staged.shape[:2]
    parts = [(f1, slot) for f1 in range(RADIX - 1) for slot in range(slots)]
    copies = []
    for i, (f1, slot) in enumerate(parts):
        copies.append(pltpu.make_async_copy(early_ref.at[f1, slot], out_hbm.at[slot, :, f1], out_sem.at[i]))
        copies[-1].start()
    halves = [spectra_ref.at[half] for half in range(HALVES)]
    for slot in range(slots):
        found, rows, cols = find_tile(slot_ref, blocks_ref, t * slots + slot)

        @pl.when(found > 0)
        def _():
            for j in range(step):
                left, right = [
                    jnp.concatenate([half[:, j, :, lanes] for half in halves], axis=0) for lanes in (rows, cols)
                ]
                total = correlate(left, right)
                staged[slot, j, 0] = total[:, :BLOCK]
                staged[slot, j, 1] = total[:, BLOCK:]

        @pl.when(found == 0)
        def _():
            staged[slot] = jnp.zeros(staged.shape[1:], jnp.float32)

        copies.append(
            pltpu.make_async_copy(staged.at[slot], out_hbm.at[slot, :, RADIX - 1], out_sem.at[len(parts) + slot])
        )
        copies[-1].start()
    for copy in copies:
        copy.wait()


def last_tiles(early, spectra, tile_slot, tile_blocks):
    slots = early.shape[1]
    smem = pl.BlockSpec(memory_space=pltpu.SMEM)
    any_space = pl.BlockSpec(memory_space=pl.ANY)
    return pl.pallas_call(
        tile_kernel,
        out_shape=jax.ShapeDtypeStruct((slots, 8, RADIX, 2, BLOCK, BLOCK), jnp.float32),
        in_specs=[smem, smem, any_space, pl.BlockSpec(memory_space=pltpu.VMEM)],
        out_specs=any_space,
        scratch_shapes=[
            pltpu.VMEM((slots, 8, 2, BLOCK, BLOCK), jnp.float32),
            pltpu.SemaphoreType.DMA((RADIX * slots,)),
        ],
        compiler_params=pltpu.CompilerParams(vmem_limit_bytes=LAST_LIMIT),
        name="tiles",
    )(*in_hbm(tile_slot, tile_blocks), early, spectra)


def solution(mesh):
    chans, tiles = mesh.shape["chan"], mesh.shape["tile"]

    def body(voltage, fir_taps, tile_slot, tile_blocks):
        channels = voltage.shape[3]
        spectra_total = voltage.shape[1] * tiles
        slots = -(-tile_slot.shape[0] // tiles)
        blocks = tile_blocks.T
        tables = jnp.asarray(dft_tables(channels, 1.0 / math.sqrt(channels * spectra_total)))
        early, last = early_tiles(voltage, fir_taps, tables, tile_slot, blocks, chans, tiles, slots)
        out = last_tiles(early, last, tile_slot, blocks)
        return out.reshape(slots, 8 * RADIX, 2, BLOCK, BLOCK)

    in_specs = (P(None, "tile", "chan", None), P(), P(), P())
    out_specs = P("tile", "chan", None, None, None)
    return jax.shard_map(body, mesh=mesh, in_specs=in_specs, out_specs=out_specs, check_vma=False)
```
